32 devices in a mesh: dp: 4 (over z), seq: 8 (over y, x, core).
Axes of the slice: x: 2, y: 2, z: 4, core: 2. Of those that a mesh axis runs over, the one named last changes fastest.
Arguments:
- frames_in: bfloat16 [4, 4096, 1024], P('dp', 'seq'), may hold values from -16 to 16
- memory_in: bfloat16 [4, 32, 1024], P('dp', 'seq'), may hold values from -6 to 6
- w_query: bfloat16 [1024, 1024], P(None, 'dp'), may hold values from -1 to 1
- w_key: bfloat16 [1024, 1024], P(None, 'dp'), may hold values from -1 to 1
- w_value: bfloat16 [1024, 1024], P(None, 'dp'), may hold values from -0.1875 to 0.1875
- lengths: int32 [4], P('dp'), may hold values from 1024 to 4096, as said below
Outputs:
- context: bfloat16 [4, 4096, 1024], P('dp', 'seq')
- memory_out: bfloat16 [4, 32, 1024], P('dp', 'seq')
The draws below stay inside these ranges and needn't reach their ends.
Inputs may be any that keep to these rules, and one draw needn't show every extreme that they name: `lengths`: some utterance has all 4096 frames live; every utterance has at least a quarter of them.
All inputs are finite; a program needn't handle non-finite values.
Results may differ from the reference program's by a relative error of at most 0.0071.
Values may be sent and summed in bfloat16 or wider, within the bound.
No kernel may reach another device: no remote copies, remote signals or barrier semaphores. Data moves between devices by JAX's collectives and lax.ppermute only.
A program may use at most 64 MiB of HBM per device.

```python
import jax
import jax.numpy as jnp
from jax import lax

D = 1024
HEADS = 16
HD = 64
SEG = 128
LEFT = 128
RIGHT = 32
BATCH = 4
NSEG = 32
FRAMES = 4096


def shared_weight(key, salt):
    own = jax.random.normal(jax.random.fold_in(key, salt), (D, D), jnp.float32)
    mixed = own / jnp.sqrt(1.0 * D)
    return jnp.clip(mixed, -0.99, 0.99)


def draw_w_query(key, part):
    return shared_weight(key, 11).astype(jnp.bfloat16)


def draw_w_key(key, part):
    return shared_weight(key, 12).astype(jnp.bfloat16)


def draw_frames_in(key, part):
    shape = (BATCH, FRAMES, D)
    values = jnp.clip(jax.random.normal(jax.random.fold_in(key, 21), shape, jnp.float32), -6.0, 6.0)
    return values.astype(jnp.bfloat16)


def draw_lengths(key, part):
    drawn = jax.random.randint(jax.random.fold_in(key, 31), (BATCH,), FRAMES // 4, FRAMES + 1, jnp.int32)
    return drawn.at[0].set(FRAMES)


def block_levels(rng, dims, shards, low, largest):
    def one(dim, blocks):
        heights = jax.random.uniform(jax.random.fold_in(jax.random.fold_in(rng, 6), dim), (blocks,), jnp.float32, low / len(shards), largest / len(shards))
        return jnp.repeat(jnp.exp(heights), dims[dim] // blocks).reshape((-1,) + (1,) * (len(dims) - dim - 1))

    factor_of = one(*shards[0])
    for cut in shards[1:]:
        factor_of = factor_of * one(*cut)
    return factor_of


def scatter_about(stream_key, dims, width, limit, pieces=(), held_as=jnp.bfloat16):
    values = jax.random.normal(stream_key, dims, jnp.float32) * width
    if len(pieces) > 0:
        values = block_levels(stream_key, dims, pieces, -0.22, 0.18) * values
    return jnp.clip(values, min=-limit, max=limit).astype(held_as)


def setup_inputs(seed: int = 0) -> dict:
    arg_keys = jax.random.split(jax.random.key(seed), 7)
    frames_in = draw_frames_in(jax.random.fold_in(arg_keys[6], 71), 0)
    memory_in = scatter_about(arg_keys[1], (BATCH, NSEG, D), 1.0, 6.0, ((0, 4), (1, 8)))
    w_query = draw_w_query(jax.random.fold_in(arg_keys[6], 71), 0)
    w_key = draw_w_key(jax.random.fold_in(arg_keys[6], 71), 0)
    w_value = scatter_about(arg_keys[4], (D, D), D ** -0.5, 0.1875, ((1, 4),))
    lengths = draw_lengths(jax.random.fold_in(arg_keys[6], 71), 0)
    return dict(frames_in=frames_in, memory_in=memory_in, w_query=w_query, w_key=w_key, w_value=w_value, lengths=lengths)


def attend(queries, keys, values, key_live, scale):
    n_query = queries.shape[0]
    n_key = keys.shape[0]
    q_heads = queries.reshape(n_query, HEADS, -1).astype(jnp.float32)
    k_heads = keys.reshape(n_key, HEADS, -1).astype(jnp.float32)
    v_heads = values.reshape(n_key, HEADS, -1).astype(jnp.float32)
    scores = jnp.einsum("qhe,khe->hqk", q_heads, k_heads) * scale
    scores = jnp.where(key_live[None, None, :], scores, -1e30)
    row_max = jnp.max(scores, axis=-1, keepdims=True)
    probs = jnp.exp(scores - row_max)
    weights = (probs / jnp.sum(probs, axis=-1, keepdims=True)).astype(jnp.bfloat16)
    mixed = jnp.einsum("hqk,khe->qhe", weights.astype(jnp.float32), v_heads)
    return mixed.reshape(n_query, -1)


def reference(frames_in, memory_in, w_query, w_key, w_value, lengths):
    scale = float(HD) ** -0.5
    key_span = LEFT + SEG + RIGHT

    def one_utterance(inputs):
        frames, bank, length = inputs
        queries = jnp.dot(frames, w_query, preferred_element_type=jnp.float32).astype(jnp.bfloat16)
        keys = jnp.dot(frames, w_key, preferred_element_type=jnp.float32).astype(jnp.bfloat16)
        values = jnp.dot(frames, w_value, preferred_element_type=jnp.float32).astype(jnp.bfloat16)
        positions = jnp.arange(FRAMES, dtype=jnp.int32).reshape(NSEG, SEG)
        live_mask = (positions < length).astype(jnp.float32)
        masked_sums = jnp.einsum("nsd,ns->nd", frames.reshape(NSEG, SEG, D).astype(jnp.float32), live_mask)
        counts = jnp.sum(live_mask, axis=1)
        summary = (masked_sums / jnp.maximum(counts, 1.0)[:, None]).astype(jnp.bfloat16)
        sum_queries = jnp.dot(summary, w_query, preferred_element_type=jnp.float32).astype(jnp.bfloat16)
        bank_keys = jnp.dot(bank, w_key, preferred_element_type=jnp.float32).astype(jnp.bfloat16)
        bank_values = jnp.dot(bank, w_value, preferred_element_type=jnp.float32).astype(jnp.bfloat16)
        keys_pad = jnp.pad(keys, ((LEFT, RIGHT), (0, 0)))
        values_pad = jnp.pad(values, ((LEFT, RIGHT), (0, 0)))
        bank_index = jnp.arange(NSEG, dtype=jnp.int32)
        bank_ready = bank_index * SEG < length

        def one_segment(seg_index):
            q_rows = lax.dynamic_slice_in_dim(queries, seg_index * SEG, SEG, 0)
            q_sum = lax.dynamic_slice_in_dim(sum_queries, seg_index, 1, 0)
            q_all = jnp.concatenate([q_rows, q_sum], axis=0)
            k_window = lax.dynamic_slice_in_dim(keys_pad, seg_index * SEG, key_span, 0)
            v_window = lax.dynamic_slice_in_dim(values_pad, seg_index * SEG, key_span, 0)
            frame_pos = seg_index * SEG - LEFT + jnp.arange(key_span, dtype=jnp.int32)
            key_live = jnp.concatenate([bank_ready & (bank_index < seg_index), (frame_pos >= 0) & (frame_pos < length)])
            return attend(q_all, jnp.concatenate([bank_keys, k_window]), jnp.concatenate([bank_values, v_window]), key_live, scale)

        attended = lax.map(one_segment, jnp.arange(NSEG, dtype=jnp.int32))
        context = (attended[:, :SEG].reshape(FRAMES, D) * live_mask.reshape(FRAMES)[:, None]).astype(jnp.bfloat16)
        return context, attended[:, SEG].astype(jnp.bfloat16)

    context, memory_out = lax.map(one_utterance, (frames_in, memory_in, lengths))
    return context, memory_out
```

```python
import jax
import jax.numpy as jnp
from jax import lax
from jax.experimental import pallas as pl
from jax.experimental.pallas import tpu as pltpu
from jax.sharding import PartitionSpec as P

HEADS = 16
LEFT = 128
RIGHT = 32
LANES = 128
PAD_ROWS = 16
DEAD = -1e30


def shifted(block, axis, distance):
    count = lax.axis_size(axis)
    route = [(i - distance, i) for i in range(count) if 0 <= i - distance < count]
    return lax.ppermute(block, axis, route)


def swapped(block, axis, masks):
    count = lax.axis_size(axis)
    return lax.ppermute(block, axis, [(i, i ^ masks[i % 2]) for i in range(count)])


def stage_masks(count):
    bits = [1 << b for b in range(1, count.bit_length() - 1)]
    turned = bits[1:] + bits[:1]
    return [pair for pair in zip(bits, turned)] + [(1, 1)]


def gather_slices(mine, axis):
    index = lax.axis_index(axis)
    odd = index % 2
    buffers = [mine[None]]
    owners = [(0, 0)]
    for even_mask, odd_mask in stage_masks(lax.axis_size(axis)):
        sent = buffers[0] if len(buffers) == 1 else jnp.concatenate(buffers, axis=0)
        buffers.append(swapped(sent, axis, (even_mask, odd_mask)))
        if even_mask == 1:
            owners = owners + [(o ^ 1, e ^ 1) for e, o in owners]
        else:
            owners = owners + [(e ^ even_mask, o ^ odd_mask) for e, o in owners]
    slots = [index ^ jnp.where(odd == 1, o, e) for e, o in owners]
    return buffers, slots


def gather_bank(memory_in, axis):
    index = lax.axis_index(axis)
    count = lax.axis_size(axis)
    bank = memory_in
    bit = 1
    while bit < count:
        bank = jnp.concatenate([bank, swapped(bank, axis, (bit, bit))], axis=1)
        bit *= 2
    return bank, index


def make_kernel(dims, first, slot_counts):
    utts, rows, feat, cols, segs, seg_len, bank_n = dims
    hd = feat // HEADS
    per_tile = LANES // hd
    span = LEFT + seg_len + RIGHT
    kv_rows = bank_n + LEFT + rows + RIGHT
    q_base = bank_n + LEFT
    q_rows = rows + RIGHT + PAD_ROWS
    scale = float(hd) ** (-0.5)

    def kernel(*refs):
        refs = list(refs)
        scal_ref = refs.pop(0)
        len_ref = refs.pop(0)
        if first:
            frames_ref, left_ref, right_ref, bank_ref = refs[:4]
            refs = refs[4:]
            w_refs = refs[:3]
            refs = refs[3:]
            ctx_ref, mem_ref, x_ref = refs[:3]
            refs = refs[3:]
        else:
            x_ref = refs.pop(0)
            w_refs = refs[: len(slot_counts)]
            refs = refs[len(slot_counts) + 2 :]
            ctx_ref, mem_ref = refs[:2]
            refs = refs[2:]
        k_scr, v_scr, q_scr, o_scr, m_scr, in_sem, out_sem = refs
        col = scal_ref[0]
        seq_index = scal_ref[1]
        row_base = seq_index * rows

        if first:
            copies = []
            for u in range(utts):
                for n, (src, at, size) in enumerate(
                    (
                        (bank_ref, 0, bank_n),
                        (left_ref, bank_n, LEFT),
                        (frames_ref, q_base, rows),
                        (right_ref, q_base + rows, RIGHT),
                    )
                ):
                    copies.append(
                        pltpu.make_async_copy(
                            src.at[u], x_ref.at[u, pl.ds(at, size)], in_sem.at[u, n]
                        )
                    )
            for c in copies:
                c.start()
            for c in copies:
                c.wait()
            for u in range(utts):
                length = len_ref[u]
                seg_of = lax.broadcasted_iota(jnp.int32, (PAD_ROWS, rows), 0)
                pos = lax.broadcasted_iota(jnp.int32, (PAD_ROWS, rows), 1)
                pick = (pos // seg_len == seg_of) & (row_base + pos < length)
                own = x_ref[u, q_base : q_base + rows, :]
                sums = jnp.dot(
                    jnp.where(pick, 1.0, 0.0).astype(jnp.bfloat16),
                    own,
                    preferred_element_type=jnp.float32,
                )
                seg = lax.broadcasted_iota(jnp.int32, (PAD_ROWS, 1), 0)
                count = jnp.clip(length - (row_base + seg * seg_len), 1, seg_len)
                mean = sums / count.astype(jnp.float32)
                x_ref[u, q_base + rows + RIGHT :, :] = mean.astype(jnp.bfloat16)

        lane = lax.broadcasted_iota(jnp.int32, (1, LANES), 1)
        waits = []
        for u in range(utts):
            length = len_ref[u]

            def project(which, lo, size):
                if first or len(slot_counts) == 1 and slot_counts[0] == 0:
                    w = w_refs[which][...] if first else w_refs[0][which]
                    return jnp.dot(
                        x_ref[u, lo : lo + size, :], w, preferred_element_type=jnp.float32
                    )
                flat = [(b, n) for b, c in enumerate(slot_counts) for n in range(c)]
                per = feat // len(flat)
                acc = None
                for t in range(0, len(flat), 2):
                    lhs = []
                    rhs = []
                    for s in (t, t + 1):
                        b, n = flat[s]
                        at = pl.multiple_of(scal_ref[2 + s] * per, LANES)
                        lhs.append(x_ref[u, lo : lo + size, pl.ds(at, per)])
                        rhs.append(w_refs[b][n, which])
                    part = jnp.dot(
                        jnp.concatenate(lhs, axis=1),
                        jnp.concatenate(rhs, axis=0),
                        preferred_element_type=jnp.float32,
                    )
                    acc = part if acc is None else acc + part
                return acc

            k_scr[u] = project(1, 0, kv_rows).astype(jnp.bfloat16)
            v_scr[u] = project(2, 0, kv_rows).astype(jnp.bfloat16)
            q_scr[u] = project(0, q_base, q_rows).astype(jnp.bfloat16)
            n_key = bank_n + span
            key_at = lax.broadcasted_iota(jnp.int32, (1, n_key), 1)
            per_dev = segs
            owner = seq_index ^ (key_at // per_dev)
            entry = owner * per_dev + key_at % per_dev
            for s in range(segs):
                seg_index = seq_index * segs + s
                pos = row_base + s * seg_len - LEFT + (key_at - bank_n)
                bank_live = (key_at < bank_n) & (entry < seg_index) & (entry * seg_len < length)
                frame_live = (key_at >= bank_n) & (pos >= 0) & (pos < length)
                bias = jnp.where(bank_live | frame_live, 0.0, DEAD)
                row_at = lax.broadcasted_iota(jnp.int32, (seg_len, 1), 0)
                row_live = (row_base + s * seg_len + row_at) < length
                for p in range(cols // LANES):
                    at = p * LANES
                    win = bank_n + s * seg_len
                    kw = jnp.concatenate(
                        [
                            k_scr[u, :bank_n, at : at + LANES],
                            k_scr[u, win : win + span, at : at + LANES],
                        ],
                        axis=0,
                    )
                    vw = jnp.concatenate(
                        [
                            v_scr[u, :bank_n, at : at + LANES],
                            v_scr[u, win : win + span, at : at + LANES],
                        ],
                        axis=0,
                    )
                    q = jnp.concatenate(
                        [
                            q_scr[u, s * seg_len : (s + 1) * seg_len, at : at + LANES],
                            q_scr[u, rows + RIGHT :, at : at + LANES],
                        ],
                        axis=0,
                    )
                    n_q = seg_len + PAD_ROWS
                    zero = jnp.zeros_like(q)
                    heads = [
                        jnp.where((lane >= h * hd) & (lane < (h + 1) * hd), q, zero)
                        for h in range(per_tile)
                    ]
                    scores = lax.dot_general(
                        jnp.concatenate(heads, axis=0),
                        kw,
                        (((1,), (1,)), ((), ())),
                        preferred_element_type=jnp.float32,
                    )
                    scores = scores * scale + bias
                    top = jnp.max(scores, axis=-1, keepdims=True)
                    probs = jnp.exp(scores - top)
                    total = jnp.sum(probs, axis=-1, keepdims=True)
                    mixed = jnp.dot(
                        probs.astype(jnp.bfloat16), vw, preferred_element_type=jnp.float32
                    )
                    mixed = mixed / total
                    out = mixed[:n_q]
                    for h in range(1, per_tile):
                        out = jnp.where(lane >= h * hd, mixed[h * n_q : (h + 1) * n_q], out)
                    live_rows = jnp.where(row_live, out[:seg_len], 0.0)
                    o_scr[u, s * seg_len : (s + 1) * seg_len, at : at + LANES] = live_rows.astype(
                        jnp.bfloat16
                    )
                    m_scr[u, s : s + 1, at : at + LANES] = out[seg_len + s : seg_len + s + 1]
                done = pltpu.make_async_copy(
                    o_scr.at[u, pl.ds(s * seg_len, seg_len)],
                    ctx_ref.at[u, pl.ds(s * seg_len, seg_len), pl.ds(pl.multiple_of(col * cols, LANES), cols)],
                    out_sem.at[u, s],
                )
                done.start()
                waits.append(done)
        mem_ref[...] = m_scr[...].astype(jnp.bfloat16)
        for done in waits:
            done.wait()

    return kernel


def attend_chunk(dims, first, scal, lengths, inputs, weights, previous):
    utts, rows, feat, cols, segs, seg_len, bank_n = dims
    kv_rows = bank_n + LEFT + rows + RIGHT
    q_rows = rows + RIGHT + PAD_ROWS
    x_rows = kv_rows + PAD_ROWS
    slot_counts = () if first else tuple(w.shape[0] for w in weights)
    if not first and weights[0].ndim == 3:
        slot_counts = (0,)
    anywhere = pl.BlockSpec(memory_space=pl.ANY)
    whole = pl.BlockSpec(memory_space=pltpu.VMEM)
    mem_block = pl.BlockSpec((utts, segs, cols), lambda i, s, n: (0, 0, s[0]))
    ctx_shape = jax.ShapeDtypeStruct((utts, rows, feat), jnp.bfloat16)
    mem_shape = jax.ShapeDtypeStruct((utts, segs, feat), jnp.bfloat16)
    if first:
        in_specs = [anywhere] * 4 + [whole] * len(weights)
        args = list(inputs) + list(weights)
        out_specs = [anywhere, mem_block, whole]
        out_shape = [
            ctx_shape,
            mem_shape,
            jax.ShapeDtypeStruct((utts, x_rows, feat), jnp.bfloat16),
        ]
        aliases = {}
    else:
        in_specs = [whole] * (1 + len(weights)) + [anywhere] * 2
        args = list(inputs) + list(weights) + list(previous)
        out_specs = [anywhere, mem_block]
        out_shape = [ctx_shape, mem_shape]
        aliases = {len(args): 0, len(args) + 1: 1}
    return pl.pallas_call(
        make_kernel(dims, first, slot_counts),
        grid_spec=pltpu.PrefetchScalarGridSpec(
            num_scalar_prefetch=2,
            grid=(1,),
            in_specs=in_specs,
            out_specs=out_specs,
            scratch_shapes=[
                pltpu.VMEM((utts, kv_rows, cols), jnp.bfloat16),
                pltpu.VMEM((utts, kv_rows, cols), jnp.bfloat16),
                pltpu.VMEM((utts, q_rows, cols), jnp.bfloat16),
                pltpu.VMEM((utts, rows, cols), jnp.bfloat16),
                pltpu.VMEM((utts, segs, cols), jnp.float32),
                pltpu.SemaphoreType.DMA((utts, 4)),
                pltpu.SemaphoreType.DMA((utts, segs)),
            ],
        ),
        out_shape=out_shape,
        input_output_aliases=aliases,
        compiler_params=pltpu.CompilerParams(vmem_limit_bytes=20 * 1024 * 1024),
        name="attend_first" if first else "attend_next",
    )(scal, lengths, *args)


def local(frames_in, memory_in, w_query, w_key, w_value, lengths):
    utts, rows, feat = frames_in.shape
    segs = memory_in.shape[1]
    seg_len = rows // segs
    seq_count = lax.axis_size("seq")
    dp_count = lax.axis_size("dp")
    seq_index = lax.axis_index("seq")
    dp_index = lax.axis_index("dp")
    bank_n = segs * seq_count
    part = feat // seq_count
    sliced = part % LANES == 0 and w_query.shape[1] % LANES == 0
    cols = w_query.shape[1] if sliced else feat // 4
    dims = (utts, rows, feat, cols, segs, seg_len, bank_n)

    later = []
    if sliced:
        mine = jnp.stack(
            [
                lax.dynamic_slice_in_dim(w, seq_index * part, part, 0)
                for w in (w_query, w_key, w_value)
            ]
        )
        arrived = [
            lax.ppermute(mine, "dp", [(i, i ^ r) for i in range(dp_count)])
            for r in range(1, dp_count)
        ]
        for r in range(1, dp_count):
            buffers, slots = gather_slices(arrived[r - 1], "seq")
            later.append((dp_index ^ r, slots, buffers))
        own = (dp_index, (w_query, w_key, w_value))
    else:
        full = [lax.all_gather(w, "dp", axis=1, tiled=True) for w in (w_query, w_key, w_value)]
        chunks = [
            (c, [w[:, c * cols : (c + 1) * cols] for w in full]) for c in range(feat // cols)
        ]
        own = chunks[0]
        later = [(c, [], [jnp.stack(ws)]) for c, ws in chunks[1:]]

    left = shifted(frames_in[:, rows - LEFT :], "seq", 1)
    right = shifted(frames_in[:, :RIGHT], "seq", -1)
    bank, _ = gather_bank(memory_in, "seq")

    def scalars(source, slots):
        return jnp.stack([jnp.asarray(v, jnp.int32) for v in [source, seq_index] + list(slots)])

    context, memory_out, x_all = attend_chunk(
        dims,
        True,
        scalars(own[0], []),
        lengths,
        (frames_in, left, right, bank),
        own[1],
        (),
    )
    for source, slots, buffers in later:
        context, memory_out = attend_chunk(
            dims, False, scalars(source, slots), lengths, (x_all,), buffers, (context, memory_out)
        )
    return context, memory_out


def solution(mesh):
    placed = (
        P("dp", "seq", None),
        P("dp", "seq", None),
        P(None, "dp"),
        P(None, "dp"),
        P(None, "dp"),
        P("dp"),
    )
    return jax.shard_map(
        local,
        mesh=mesh,
        in_specs=placed,
        out_specs=(P("dp", "seq", None), P("dp", "seq", None)),
        check_vma=False,
    )
```

```python
import jax
import jax.numpy as jnp
from jax import lax
from jax.experimental import pallas as pl
from jax.experimental.pallas import tpu as pltpu
from jax.sharding import PartitionSpec as P


HEADS = 16
LEFT = 128
RIGHT = 32
LANES = 128
PAD_ROWS = 16
DEAD = -1e30
MIB = 1024 * 1024


def shifted(block, axis, distance):
    count = lax.axis_size(axis)
    route = [(i - distance, i) for i in range(count) if 0 <= i - distance < count]
    return lax.ppermute(block, axis, route)


def swapped(block, axis, masks):
    count = lax.axis_size(axis)
    return lax.ppermute(block, axis, [(i, i ^ masks[i % 2]) for i in range(count)])


def stage_masks(count):
    bits = [1 << b for b in range(1, count.bit_length() - 1)]
    turned = bits[1:] + bits[:1]
    return [pair for pair in zip(bits, turned)] + [(1, 1)]


def gather_slices(mine, axis):
    index = lax.axis_index(axis)
    blocks = [(mine[None], [(0, 0)])]
    for even_mask, odd_mask in stage_masks(lax.axis_size(axis)):
        if even_mask == 1:
            for block, owners in list(blocks):
                got = swapped(block, axis, (1, 1))
                blocks.append((got, [(o ^ 1, e ^ 1) for e, o in owners]))
            break
        owners = [pair for block in blocks for pair in block[1]]
        sent = blocks[0][0]
        if len(blocks) > 1:
            sent = jnp.concatenate([block[0] for block in blocks], axis=0)
        got = swapped(sent, axis, (even_mask, odd_mask))
        blocks = [(sent, owners), (got, [(e ^ even_mask, o ^ odd_mask) for e, o in owners])]
    odd = index % 2 == 1
    slots = [index ^ jnp.where(odd, o, e) for block in blocks for e, o in block[1]]
    return [block[0] for block in blocks], slots


def gather_bank(memory_in, axis):
    count = lax.axis_size(axis)
    bank = memory_in
    bit = 1
    while bit < count:
        bank = jnp.concatenate([bank, swapped(bank, axis, (bit, bit))], axis=1)
        bit *= 2
    return bank


def cut(seq_index, part, frames_in, weights):
    utts, rows, feat = frames_in.shape
    cols = weights[0].shape[1]

    def kernel(scal_ref, f_ref, *refs):
        w_refs = refs[:3]
        u_ref, last_ref, head_ref, sem = refs[3:]
        at = pl.multiple_of(scal_ref[0] * part, part)
        copies = [
            pltpu.make_async_copy(w.at[pl.ds(at, part)], u_ref.at[n], sem.at[n])
            for n, w in enumerate(w_refs)
        ]
        copies.append(
            pltpu.make_async_copy(f_ref.at[:, pl.ds(rows - LEFT, LEFT)], last_ref, sem.at[3])
        )
        copies.append(pltpu.make_async_copy(f_ref.at[:, pl.ds(0, RIGHT)], head_ref, sem.at[4]))
        for c in copies:
            c.start()
        for c in copies:
            c.wait()

    hbm = pl.BlockSpec(memory_space=pltpu.HBM)
    local = pl.BlockSpec(memory_space=pltpu.VMEM)
    return pl.pallas_call(
        kernel,
        in_specs=[pl.BlockSpec(memory_space=pltpu.SMEM)] + [hbm] * 4,
        out_specs=[local] * 3,
        out_shape=[
            jax.ShapeDtypeStruct((3, part, cols), jnp.bfloat16),
            jax.ShapeDtypeStruct((utts, LEFT, feat), jnp.bfloat16),
            jax.ShapeDtypeStruct((utts, RIGHT, feat), jnp.bfloat16),
        ],
        scratch_shapes=[pltpu.SemaphoreType.DMA((5,))],
        compiler_params=pltpu.CompilerParams(vmem_limit_bytes=4 * MIB),
        name="cut",
    )(
        jnp.reshape(seq_index, (1,)),
        *[pltpu.with_memory_space_constraint(a, pltpu.HBM) for a in (frames_in, *weights)],
    )


def make_kernel(dims, first, slot_counts):
    utts, rows, feat, cols, segs, seg_len, bank_n = dims
    hd = feat // HEADS
    per_tile = LANES // hd
    span = LEFT + seg_len + RIGHT
    kv_rows = bank_n + LEFT + rows + RIGHT
    q_base = bank_n + LEFT
    q_rows = rows + RIGHT + PAD_ROWS
    scale = float(hd) ** (-0.5)
    half = kv_rows // 2 // PAD_ROWS * PAD_ROWS

    def kernel(*refs):
        refs = list(refs)
        scal_ref = refs.pop(0)
        len_ref = refs.pop(0)
        if first:
            frames_ref, left_ref, right_ref, bank_ref = refs[:4]
            w_hbm = refs[4:7]
            ctx_ref, mem_ref, x_hbm = refs[7:10]
            k_scr, v_scr, q_scr, o_scr, m_scr, out_sem, x_ref, w_scr, in_sem = refs[10:]
        else:
            x_hbm = refs.pop(0)
            w_refs = refs[: len(slot_counts)]
            refs = refs[len(slot_counts) + 2 :]
            ctx_ref, mem_ref = refs[:2]
            k_scr, v_scr, q_scr, o_scr, m_scr, out_sem, x_ref, in_sem = refs[2:]
        seq_index = scal_ref[0]
        col_at = pl.multiple_of(scal_ref[1] * cols, cols)
        row_base = seq_index * rows
        waits = []

        if first:
            copies = []
            for u in range(utts):
                for n, (src, at, size) in enumerate(
                    (
                        (bank_ref, 0, bank_n),
                        (left_ref, bank_n, LEFT),
                        (frames_ref, q_base, rows),
                        (right_ref, q_base + rows, RIGHT),
                    )
                ):
                    copies.append(
                        pltpu.make_async_copy(
                            src.at[u], x_ref.at[u, pl.ds(at, size)], in_sem.at[3 + 4 * u + n]
                        )
                    )
            copies += [
                pltpu.make_async_copy(w_hbm[n], w_scr.at[n], in_sem.at[n]) for n in range(3)
            ]
            for c in copies:
                c.start()
            for c in copies[:-3]:
                c.wait()
            arriving = {n: copies[n - 3] for n in range(3)}
            for u in range(utts):
                length = len_ref[u]
                seg_of = lax.broadcasted_iota(jnp.int32, (PAD_ROWS, rows), 0)
                pos = lax.broadcasted_iota(jnp.int32, (PAD_ROWS, rows), 1)
                pick = (pos // seg_len == seg_of) & (row_base + pos < length)
                own = x_ref[u, q_base : q_base + rows, :]
                sums = jnp.dot(
                    jnp.where(pick, 1.0, 0.0).astype(jnp.bfloat16),
                    own,
                    preferred_element_type=jnp.float32,
                )
                seg = lax.broadcasted_iota(jnp.int32, (PAD_ROWS, 1), 0)
                count = jnp.clip(length - (row_base + seg * seg_len), 1, seg_len)
                mean = sums / count.astype(jnp.float32)
                x_ref[u, q_base + rows + RIGHT :, :] = mean.astype(jnp.bfloat16)
            done = pltpu.make_async_copy(x_ref, x_hbm, in_sem.at[3])
            done.start()
            waits.append(done)
        else:
            pieces = []
            for u in range(utts):
                for n, (lo, hi) in enumerate(((0, half), (half, kv_rows + PAD_ROWS))):
                    pieces.append(
                        pltpu.make_async_copy(
                            x_hbm.at[u, pl.ds(lo, hi - lo)],
                            x_ref.at[u, pl.ds(lo, hi - lo)],
                            in_sem.at[2 * u + n],
                        )
                    )
            for c in pieces:
                c.start()

        lane = lax.broadcasted_iota(jnp.int32, (1, LANES), 1)
        for u in range(utts):
            length = len_ref[u]

            def project(which, lo, size):
                if first or slot_counts == (0,):
                    w = w_scr[which] if first else w_refs[0][which]
                    return jnp.dot(
                        x_ref[u, lo : lo + size, :], w, preferred_element_type=jnp.float32
                    )
                flat = [(b, n) for b, c in enumerate(slot_counts) for n in range(c)]
                per = feat // len(flat)
                acc = None
                for t in range(0, len(flat), 2):
                    lhs = []
                    rhs = []
                    for s in (t, t + 1):
                        b, n = flat[s]
                        at = pl.multiple_of(scal_ref[2 + s] * per, LANES)
                        lhs.append(x_ref[u, lo : lo + size, pl.ds(at, per)])
                        rhs.append(w_refs[b][n, which])
                    part = jnp.dot(
                        jnp.concatenate(lhs, axis=1),
                        jnp.concatenate(rhs, axis=0),
                        preferred_element_type=jnp.float32,
                    )
                    acc = part if acc is None else acc + part
                return acc

            if first:
                if u == 0:
                    arriving[1].wait()
                k_scr[u] = project(1, 0, kv_rows).astype(jnp.bfloat16)
            else:
                pieces[2 * u].wait()
                k_scr[u, :half] = project(1, 0, half).astype(jnp.bfloat16)
                pieces[2 * u + 1].wait()
                k_scr[u, half:] = project(1, half, kv_rows - half).astype(jnp.bfloat16)
            if first and u == 0:
                arriving[2].wait()
            v_scr[u] = project(2, 0, kv_rows).astype(jnp.bfloat16)
            if first and u == 0:
                arriving[0].wait()
            q_scr[u] = project(0, q_base, q_rows).astype(jnp.bfloat16)
            n_key = bank_n + span
            key_at = lax.broadcasted_iota(jnp.int32, (1, n_key), 1)
            per_dev = segs
            owner = seq_index ^ (key_at // per_dev)
            entry = owner * per_dev + key_at % per_dev
            for s in range(segs):
                seg_index = seq_index * segs + s
                pos = row_base + s * seg_len - LEFT + (key_at - bank_n)
                bank_live = (key_at < bank_n) & (entry < seg_index) & (entry * seg_len < length)
                frame_live = (key_at >= bank_n) & (pos >= 0) & (pos < length)
                bias = jnp.where(bank_live | frame_live, 0.0, DEAD)
                row_at = lax.broadcasted_iota(jnp.int32, (seg_len, 1), 0)
                row_live = (row_base + s * seg_len + row_at) < length
                for p in range(cols // LANES):
                    at = p * LANES
                    win = bank_n + s * seg_len
                    kw = jnp.concatenate(
                        [
                            k_scr[u, :bank_n, at : at + LANES],
                            k_scr[u, win : win + span, at : at + LANES],
                        ],
                        axis=0,
                    )
                    vw = jnp.concatenate(
                        [
                            v_scr[u, :bank_n, at : at + LANES],
                            v_scr[u, win : win + span, at : at + LANES],
                        ],
                        axis=0,
                    )
                    q = jnp.concatenate(
                        [
                            q_scr[u, s * seg_len : (s + 1) * seg_len, at : at + LANES],
                            q_scr[u, rows + RIGHT :, at : at + LANES],
                        ],
                        axis=0,
                    )
                    n_q = seg_len + PAD_ROWS
                    zero = jnp.zeros_like(q)
                    heads = [
                        jnp.where((lane >= h * hd) & (lane < (h + 1) * hd), q, zero)
                        for h in range(per_tile)
                    ]
                    scores = lax.dot_general(
                        jnp.concatenate(heads, axis=0),
                        kw,
                        (((1,), (1,)), ((), ())),
                        preferred_element_type=jnp.float32,
                    )
                    scores = scores * scale + bias
                    top = jnp.max(scores, axis=-1, keepdims=True)
                    probs = jnp.exp(scores - top)
                    total = jnp.sum(probs, axis=-1, keepdims=True)
                    mixed = jnp.dot(
                        probs.astype(jnp.bfloat16), vw, preferred_element_type=jnp.float32
                    )
                    mixed = mixed / total
                    out = mixed[:n_q]
                    for h in range(1, per_tile):
                        out = jnp.where(lane >= h * hd, mixed[h * n_q : (h + 1) * n_q], out)
                    live_rows = jnp.where(row_live, out[:seg_len], 0.0)
                    o_scr[u, s * seg_len : (s + 1) * seg_len, at : at + LANES] = live_rows.astype(
                        jnp.bfloat16
                    )
                    m_scr[u, s : s + 1, at : at + LANES] = out[seg_len + s : seg_len + s + 1]
                done = pltpu.make_async_copy(
                    o_scr.at[u, pl.ds(s * seg_len, seg_len)],
                    ctx_ref.at[u, pl.ds(s * seg_len, seg_len), pl.ds(col_at, cols)],
                    out_sem.at[u, s],
                )
                done.start()
                waits.append(done)
        o_scr[:, rows : rows + segs, :] = m_scr[...].astype(jnp.bfloat16)
        for u in range(utts):
            done = pltpu.make_async_copy(
                o_scr.at[u, pl.ds(rows, segs)],
                mem_ref.at[u, :, pl.ds(col_at, cols)],
                out_sem.at[u, segs],
            )
            done.start()
            waits.append(done)
        for done in waits:
            done.wait()

    return kernel


def attend_chunk(dims, first, scal, lengths, inputs, weights, previous):
    utts, rows, feat, cols, segs, _, bank_n = dims
    kv_rows = bank_n + LEFT + rows + RIGHT
    q_rows = rows + RIGHT + PAD_ROWS
    x_rows = kv_rows + PAD_ROWS
    slot_counts = () if first else tuple(w.shape[0] for w in weights)
    if not first and weights[0].ndim == 3:
        slot_counts = (0,)
    anywhere = pl.BlockSpec(memory_space=pl.ANY)
    vmem = pl.BlockSpec(memory_space=pltpu.VMEM)
    smem = pl.BlockSpec(memory_space=pltpu.SMEM)
    ctx_shape = jax.ShapeDtypeStruct((utts, rows, feat), jnp.bfloat16)
    mem_shape = jax.ShapeDtypeStruct((utts, segs, feat), jnp.bfloat16)
    if first:
        weights = [pltpu.with_memory_space_constraint(w, pltpu.HBM) for w in weights]
    else:
        inputs = [pltpu.with_memory_space_constraint(x, pltpu.HBM) for x in inputs]
    args = [scal, lengths] + list(inputs) + list(weights) + list(previous)
    scratch = [
        pltpu.VMEM((utts, kv_rows, cols), jnp.bfloat16),
        pltpu.VMEM((utts, kv_rows, cols), jnp.bfloat16),
        pltpu.VMEM((utts, q_rows, cols), jnp.bfloat16),
        pltpu.VMEM((utts, rows + PAD_ROWS, cols), jnp.bfloat16),
        pltpu.VMEM((utts, segs, cols), jnp.float32),
        pltpu.SemaphoreType.DMA((utts, segs + 1)),
        pltpu.VMEM((utts, x_rows, feat), jnp.bfloat16),
    ]
    hbm = pl.BlockSpec(memory_space=pltpu.HBM)
    if first:
        in_specs = [smem] * 2 + [anywhere] * 4 + [hbm] * 3
        out_specs = [anywhere, anywhere, hbm]
        out_shape = [
            ctx_shape,
            mem_shape,
            pltpu.HBM((utts, x_rows, feat), jnp.bfloat16),
        ]
        aliases = {}
        scratch += [
            pltpu.VMEM((3, feat, cols), jnp.bfloat16),
            pltpu.SemaphoreType.DMA((3 + 4 * utts,)),
        ]
    else:
        scratch.append(pltpu.SemaphoreType.DMA((2 * utts,)))
        in_specs = [smem] * 2 + [hbm] + [vmem] * len(weights) + [anywhere] * 2
        out_specs = [anywhere, anywhere]
        out_shape = [ctx_shape, mem_shape]
        aliases = {len(args) - 2: 0, len(args) - 1: 1}
    work = 2 * utts * (2 * kv_rows + q_rows) * feat * cols
    return pl.pallas_call(
        make_kernel(dims, first, slot_counts),
        in_specs=in_specs,
        out_specs=out_specs,
        out_shape=out_shape,
        scratch_shapes=scratch,
        input_output_aliases=aliases,
        compiler_params=pltpu.CompilerParams(vmem_limit_bytes=16 * MIB),
        cost_estimate=pl.CostEstimate(
            flops=4 * work, transcendentals=0, bytes_accessed=utts * x_rows * feat * 2
        ),
        name="attend_first" if first else "attend_next",
    )(*args)


def local(frames_in, memory_in, w_query, w_key, w_value, lengths):
    utts, rows, feat = frames_in.shape
    segs = memory_in.shape[1]
    seg_len = rows // segs
    seq_count = lax.axis_size("seq")
    dp_count = lax.axis_size("dp")
    seq_index = lax.axis_index("seq")
    dp_index = lax.axis_index("dp")
    bank_n = segs * seq_count
    part = feat // seq_count
    sliced = part % LANES == 0 and w_query.shape[1] % LANES == 0
    cols = w_query.shape[1] if sliced else feat // 4
    dims = (utts, rows, feat, cols, segs, seg_len, bank_n)

    later = []
    weights = (w_query, w_key, w_value)
    if sliced:
        mine, last, head = cut(seq_index, part, frames_in, weights)
        arrived = {0: mine}
        for r in range(1, dp_count):
            low = r & -r
            arrived[r] = swapped(arrived[r ^ low], "dp", (low, low))
        for r in range(1, dp_count):
            buffers, slots = gather_slices(arrived[r], "seq")
            later.append((dp_index ^ r, slots, buffers))
        own = (dp_index, weights)
    else:
        full = [lax.all_gather(w, "dp", axis=1, tiled=True) for w in (w_query, w_key, w_value)]
        chunks = [
            (c, [w[:, c * cols : (c + 1) * cols] for w in full]) for c in range(feat // cols)
        ]
        own = chunks[0]
        later = [(c, [], [jnp.stack(ws)]) for c, ws in chunks[1:]]
        last = frames_in[:, rows - LEFT :]
        head = frames_in[:, :RIGHT]

    left = shifted(last, "seq", 1)
    right = shifted(head, "seq", -1)
    bank = gather_bank(memory_in, "seq")

    def scalars(source, slots):
        return jnp.stack([jnp.asarray(v, jnp.int32) for v in [seq_index, source] + list(slots)])

    context, memory_out, x_all = attend_chunk(
        dims,
        True,
        scalars(own[0], []),
        lengths,
        (frames_in, left, right, bank),
        own[1],
        (),
    )
    for source, slots, buffers in later:
        context, memory_out = attend_chunk(
            dims,
            False,
            scalars(source, slots),
            lengths,
            (x_all,),
            buffers,
            (context, memory_out),
        )
    return context, memory_out


def solution(mesh):
    placed = (
        P("dp", "seq", None),
        P("dp", "seq", None),
        P(None, "dp"),
        P(None, "dp"),
        P(None, "dp"),
        P("dp"),
    )
    return jax.shard_map(
        local,
        mesh=mesh,
        in_specs=placed,
        out_specs=(P("dp", "seq", None), P("dp", "seq", None)),
        check_vma=False,
    )
```

```python
import math

import jax
import jax.numpy as jnp
from jax import lax
from jax.experimental import pallas as pl
from jax.experimental.pallas import tpu as pltpu
from jax.sharding import PartitionSpec as P


HEADS = 16
LEFT = 128
RIGHT = 32
LANES = 128
PAD_ROWS = 16
DEAD = -1e30
MIB = 1024 * 1024


def shifted(block, axis, distance):
    count = lax.axis_size(axis)
    route = [(i - distance, i) for i in range(count) if 0 <= i - distance < count]
    return lax.ppermute(block, axis, route)


def swapped(block, axis, masks):
    count = lax.axis_size(axis)
    return lax.ppermute(block, axis, [(i, i ^ masks[i % 2]) for i in range(count)])


def stage_masks(count):
    bits = [1 << b for b in range(1, count.bit_length() - 1)]
    turned = bits[1:] + bits[:1]
    return [pair for pair in zip(bits, turned)] + [(1, 1)]


def joined(parts):
    rows = sum(p.shape[0] for p in parts)
    out = jnp.zeros((rows,) + parts[0].shape[1:], parts[0].dtype)
    at = 0
    for p in parts:
        out = lax.dynamic_update_slice_in_dim(out, p, at, 0)
        at += p.shape[0]
    return out


def gather_slices(mine, axis, tail=None):
    (even_a, odd_a), (even_b, odd_b) = stage_masks(lax.axis_size(axis))[:2]
    size = mine.shape[0]
    sent = mine if tail is None else joined([mine, tail])
    got = swapped(sent, axis, (even_a, odd_a))
    both = [mine, got] if tail is None else [mine, got[:size], tail, got[size:]]
    held = joined(both)
    other = swapped(held, axis, (even_b, odd_b))
    pair_held = swapped(held, axis, (1, 1))
    pair_other = swapped(other, axis, (1, 1))
    slots = [(0, 0), (even_a, odd_a), (even_b, odd_b), (even_a ^ even_b, odd_a ^ odd_b)]
    slots += [(o ^ 1, e ^ 1) for e, o in slots]
    return [held, other, pair_held, pair_other], slots


def gather_bank(memory_in, axis):
    count = lax.axis_size(axis)
    bank = memory_in
    bit = 1
    while bit < count:
        bank = jnp.concatenate([bank, swapped(bank, axis, (bit, bit))], axis=1)
        bit *= 2
    return bank


def cut(ids, part, frames_in, memory_in, weights):
    _, rows, feat = frames_in.shape
    segs = memory_in.shape[1]
    cols = weights[0].shape[1]
    groups = feat // cols
    packed = part // groups

    def kernel(scal_ref, f_ref, m_ref, *refs):
        w_refs = refs[:3]
        u_ref, near_ref, far_ref, m_scr, sem = refs[3:]
        at = pl.multiple_of(scal_ref[0] * part, part)
        odd = scal_ref[0] % 2
        copies = []
        for n, w in enumerate(w_refs):
            for g in range(groups):
                copies.append(
                    pltpu.make_async_copy(
                        w.at[pl.ds(at + g * packed, packed)],
                        u_ref.at[pl.ds(n * packed, packed), pl.ds(g * cols, cols)],
                        sem.at[n * groups + g],
                    )
                )
        top = pl.multiple_of((rows - LEFT) * odd, PAD_ROWS)
        end = pl.multiple_of((rows - LEFT) * (1 - odd), PAD_ROWS)
        copies.append(
            pltpu.make_async_copy(
                f_ref.at[0, pl.ds(end, LEFT)], near_ref.at[pl.ds(0, LEFT)], sem.at[3 * groups]
            )
        )
        copies.append(
            pltpu.make_async_copy(f_ref.at[0, pl.ds(top, LEFT)], far_ref, sem.at[3 * groups + 1])
        )
        copies.append(pltpu.make_async_copy(m_ref.at[0], m_scr, sem.at[3 * groups + 2]))
        for c in copies:
            c.start()
        for c in copies:
            c.wait()
        near_ref[LEFT : LEFT + segs, :] = m_scr[...]
        near_ref[LEFT + segs :, :] = jnp.zeros((PAD_ROWS - segs, feat), jnp.bfloat16)

    hbm = pl.BlockSpec(memory_space=pltpu.HBM)
    vmem = pl.BlockSpec(memory_space=pltpu.VMEM)
    return pl.pallas_call(
        kernel,
        in_specs=[pl.BlockSpec(memory_space=pltpu.SMEM)] + [hbm] * 5,
        out_specs=[vmem] * 3,
        out_shape=[
            jax.ShapeDtypeStruct((3 * packed, feat), jnp.bfloat16),
            jax.ShapeDtypeStruct((LEFT + PAD_ROWS, feat), jnp.bfloat16),
            jax.ShapeDtypeStruct((LEFT, feat), jnp.bfloat16),
        ],
        scratch_shapes=[
            pltpu.VMEM((segs, feat), jnp.bfloat16),
            pltpu.SemaphoreType.DMA((3 * groups + 3,)),
        ],
        compiler_params=pltpu.CompilerParams(vmem_limit_bytes=4 * MIB),
        name="cut",
    )(ids, *[in_hbm(a) for a in (frames_in, memory_in, *weights)])


def in_hbm(a):
    return pltpu.with_memory_space_constraint(a, pltpu.HBM)


def in_vmem(a):
    return pltpu.with_memory_space_constraint(a, pltpu.VMEM)


def attend_segment(q, k_main, k_tail, v_main, v_tail, main_bias, tail_bias, hd):
    n_q, cols = q.shape
    heads = cols // hd
    tail_n = k_tail.shape[0]
    scale = float(hd) ** (-0.5)
    exact = math.frexp(scale)[0] == 0.5
    if exact:
        q = q * jnp.asarray(scale, q.dtype)
    lane_head = lax.broadcasted_iota(jnp.int32, (1, cols), 1) // hd
    tail_head = lax.broadcasted_iota(jnp.int32, (1, heads * tail_n), 1) // tail_n

    def only(a, h):
        return jnp.where(lane_head == h, a, jnp.zeros_like(a))

    def split(a):
        return [a[:, j : j + LANES] for j in range(0, a.shape[1], LANES)]

    def folded(parts, op):
        out = parts[0]
        for part in parts[1:]:
            out = op(out, part)
        return out

    across = (((1,), (1,)), ((), ()))
    main = lax.dot_general(
        jnp.concatenate([only(q, h) for h in range(heads)], axis=0),
        k_main,
        across,
        preferred_element_type=jnp.float32,
    )
    tail = lax.dot_general(
        q,
        jnp.concatenate([only(k_tail, h) for h in range(heads)], axis=0),
        across,
        preferred_element_type=jnp.float32,
    )
    if not exact:
        main = main * scale
        tail = tail * scale
    tails = split(tail + tail_bias)
    owners = split(tail_head)
    held = [
        [j for j in range(len(tails)) if j * LANES < (h + 1) * tail_n and (j + 1) * LANES > h * tail_n]
        for h in range(heads)
    ]
    tops = []
    probs = []
    for h in range(heads):
        scores = main[h * n_q : (h + 1) * n_q] + main_bias
        parts = split(scores) + [jnp.where(owners[j] == h, tails[j], DEAD) for j in held[h]]
        top = jnp.max(folded(parts, jnp.maximum), axis=-1, keepdims=True)
        tops.append(top)
        probs.append(jnp.exp(scores - top))
    tail_probs = []
    for j, block in enumerate(tails):
        inside = [h for h in range(heads) if j in held[h]]
        top = tops[inside[0]]
        for h in inside[1:]:
            top = jnp.where(owners[j] >= h, tops[h], top)
        tail_probs.append(jnp.exp(block - top))
    shares = []
    for h in range(heads):
        parts = split(probs[h]) + [jnp.where(owners[j] == h, tail_probs[j], 0.0) for j in held[h]]
        shares.append(1.0 / jnp.sum(folded(parts, jnp.add), axis=-1, keepdims=True))
    mixed = jnp.dot(
        jnp.concatenate([p.astype(jnp.bfloat16) for p in probs + tail_probs], axis=1),
        jnp.concatenate(
            [only(v_main, h) for h in range(heads)] + [only(v_tail, h) for h in range(heads)],
            axis=0,
        ),
        preferred_element_type=jnp.float32,
    )
    outs = []
    for block, head in zip(split(mixed), split(lane_head)):
        at = len(outs) * LANES
        inside = [h for h in range(heads) if at <= h * hd < at + LANES]
        share = shares[inside[0]]
        for h in inside[1:]:
            share = jnp.where(head >= h, shares[h], share)
        outs.append(block * share)
    return jnp.concatenate(outs, axis=1)


def make_kernel(dims, first, last, sliced, n_buffers, columns, bank_devices, slots):
    utts, rows, feat, cols, segs, seg_len, bank_n = dims
    hd = feat // HEADS
    heads = cols // hd
    main_n = LEFT + seg_len
    tail_n = bank_n + RIGHT
    kv_rows = bank_n + LEFT + rows + RIGHT
    q_base = bank_n + LEFT
    n_slots = len(slots)
    n_before = len(columns) - 1 if last else 0

    def kernel(*refs):
        refs = list(refs)

        def take(n):
            got = refs[:n]
            del refs[:n]
            return got

        ids_ref, len_ref = take(2)
        if first:
            (frames_ref,) = take(1)
            edges = take(4 if sliced else 3)
            w_hbm = take(3)
        else:
            (x_ref,) = take(1)
            w_refs = take(n_buffers)
        before = take(n_before)
        if last:
            ctx_ref, mem_ref = take(2)
        else:
            (o_ref,) = take(1)
        if first:
            (x_ref,) = take(1)
        k_scr, v_scr, q_scr, m_scr = take(4)
        if first:
            w_scr, in_sem = take(2)
        if last:
            o_ref, out_sem = take(2)
        seq_index = ids_ref[0]
        odd = seq_index % 2 == 1
        row_base = seq_index * rows
        waits = []

        def column(which):
            kind, value = columns[which]
            index = ids_ref[1] ^ value if kind == "xor" else value
            return pl.multiple_of(index * cols, cols)

        def device(pair):
            return seq_index ^ jnp.where(odd, pair[1], pair[0])

        def write_out(block_ref, at, u, lo, size, target, sem):
            done = pltpu.make_async_copy(
                block_ref.at[u, pl.ds(lo, size)],
                target.at[u, pl.ds(0 if target is mem_ref else lo, size), pl.ds(at, cols)],
                sem,
            )
            done.start()
            waits.append(done)

        for n, block_ref in enumerate(before):
            for u in range(utts):
                write_out(block_ref, column(n), u, 0, rows, ctx_ref, out_sem.at[u, 2 * n])
                write_out(
                    block_ref, column(n), u, rows, segs, mem_ref, out_sem.at[u, 2 * n + 1]
                )

        if first:
            loads = [pltpu.make_async_copy(w_hbm[n], w_scr.at[n], in_sem.at[n]) for n in range(3)]
            moves = [
                pltpu.make_async_copy(
                    frames_ref.at[u], x_ref.at[u, pl.ds(q_base, rows)], in_sem.at[3 + u]
                )
                for u in range(utts)
            ]
            for c in moves + [loads[1], loads[2], loads[0]]:
                c.start()
            if sliced:
                near_ref, far_ref, held_ref, other_ref = edges
                near = near_ref[:LEFT, :]
                far = far_ref[...]
                x_ref[0, bank_n:q_base, :] = jnp.where(odd, near, far)
                x_ref[0, q_base + rows : kv_rows, :] = jnp.where(odd, far[:RIGHT], near[:RIGHT])
                x_ref[0, : bank_n // 2, :] = held_ref[held_ref.shape[0] - bank_n // 2 :, :]
                x_ref[0, bank_n // 2 : bank_n, :] = other_ref[other_ref.shape[0] - bank_n // 2 :, :]
            else:
                left_ref, right_ref, bank_ref = edges
                x_ref[:, bank_n:q_base, :] = left_ref[...]
                x_ref[:, q_base + rows : kv_rows, :] = right_ref[...]
                x_ref[:, :bank_n, :] = bank_ref[...]
            for c in moves:
                c.wait()
            for u in range(utts):
                length = len_ref[u]
                seg_of = lax.broadcasted_iota(jnp.int32, (PAD_ROWS, rows), 0)
                pos = lax.broadcasted_iota(jnp.int32, (PAD_ROWS, rows), 1)
                pick = (pos // seg_len == seg_of) & (row_base + pos < length)
                sums = jnp.dot(
                    jnp.where(pick, 1.0, 0.0).astype(jnp.bfloat16),
                    x_ref[u, q_base : q_base + rows, :],
                    preferred_element_type=jnp.float32,
                )
                seg = lax.broadcasted_iota(jnp.int32, (PAD_ROWS, 1), 0)
                count = jnp.clip(length - (row_base + seg * seg_len), 1, seg_len)
                mean = sums / count.astype(jnp.float32)
                x_ref[u, kv_rows:, :] = mean.astype(jnp.bfloat16)

        tail_at = lax.broadcasted_iota(jnp.int32, (1, heads * tail_n), 1) % tail_n
        block = tail_at // segs
        entry = tail_at % segs
        for b, pair in enumerate(bank_devices):
            entry = entry + jnp.where(block == b, device(pair) * segs, 0)
        main_at = lax.broadcasted_iota(jnp.int32, (1, main_n), 1)

        for u in range(utts):
            length = len_ref[u]

            def project(which, lo, hi):
                if first or n_slots == 0:
                    if first and u == 0:
                        loads[which].wait()
                    w = w_scr[which] if first else w_refs[0][which]
                    return jnp.dot(
                        x_ref[u, lo:hi, :], w, preferred_element_type=jnp.float32
                    ).astype(jnp.bfloat16)
                part = feat // n_slots
                packed = part * cols // feat
                per = n_slots // n_buffers
                acc = None
                for t in range(0, n_slots, 2):
                    lhs = []
                    rhs = []
                    for s in (t, t + 1):
                        at = pl.multiple_of(device(slots[s]) * part, LANES)
                        lhs.append(x_ref[u, lo:hi, pl.ds(at, part)])
                        top = (s % per * 3 + which) * packed
                        for g in range(0, feat, cols):
                            rhs.append(w_refs[s // per][top : top + packed, g : g + cols])
                    one = jnp.dot(
                        jnp.concatenate(lhs, axis=1),
                        jnp.concatenate(rhs, axis=0),
                        preferred_element_type=jnp.float32,
                    )
                    acc = one if acc is None else acc + one
                return acc.astype(jnp.bfloat16)

            k_scr[u] = project(1, 0, kv_rows)
            v_scr[u] = project(2, 0, kv_rows)
            q_scr[u] = project(0, q_base, kv_rows + PAD_ROWS)
            for s in range(segs):
                seg_index = seq_index * segs + s
                start = row_base + s * seg_len
                main_pos = start - LEFT + main_at
                main_bias = jnp.where((main_pos >= 0) & (main_pos < length), 0.0, DEAD)
                bank_live = (tail_at < bank_n) & (entry < seg_index) & (entry * seg_len < length)
                right_pos = start + seg_len - bank_n + tail_at
                tail_live = bank_live | ((tail_at >= bank_n) & (right_pos < length))
                tail_bias = jnp.where(tail_live, 0.0, DEAD)
                win = bank_n + s * seg_len
                edge = win + main_n

                def keys(scr):
                    both = [scr[u, :bank_n, :], scr[u, edge : edge + RIGHT, :]]
                    return scr[u, win:edge, :], jnp.concatenate(both, axis=0)

                k_main, k_tail = keys(k_scr)
                v_main, v_tail = keys(v_scr)
                q = jnp.concatenate(
                    [q_scr[u, s * seg_len : (s + 1) * seg_len, :], q_scr[u, rows + RIGHT :, :]],
                    axis=0,
                )
                out = attend_segment(
                    q, k_main, k_tail, v_main, v_tail, main_bias, tail_bias, hd
                )
                row_at = lax.broadcasted_iota(jnp.int32, (seg_len, 1), 0)
                live = jnp.where(start + row_at < length, out[:seg_len], 0.0)
                o_ref[u, s * seg_len : (s + 1) * seg_len, :] = live.astype(jnp.bfloat16)
                m_scr[u, s : s + 1, :] = out[seg_len + s : seg_len + s + 1]
                if last:
                    write_out(
                        o_ref,
                        column(-1),
                        u,
                        s * seg_len,
                        seg_len,
                        ctx_ref,
                        out_sem.at[u, 2 * n_before + s],
                    )
            o_ref[u, rows : rows + segs, :] = m_scr[u].astype(jnp.bfloat16)
            if last:
                write_out(
                    o_ref, column(-1), u, rows, segs, mem_ref, out_sem.at[u, 2 * n_before + segs]
                )
        for done in waits:
            done.wait()

    return kernel


def attend_chunk(
    dims, sliced, first, last, scalars, inputs, weights, columns, bank_devices, slots, before=()
):
    utts, rows, feat, cols, segs, _, bank_n = dims
    kv_rows = bank_n + LEFT + rows + RIGHT
    q_rows = rows + RIGHT + PAD_ROWS
    block = (utts, rows + PAD_ROWS, cols)
    anywhere = pl.BlockSpec(memory_space=pl.ANY)
    hbm = pl.BlockSpec(memory_space=pltpu.HBM)
    vmem = pl.BlockSpec(memory_space=pltpu.VMEM)
    smem = pl.BlockSpec(memory_space=pltpu.SMEM)
    if first:
        weights = [in_hbm(w) for w in weights]
    else:
        inputs = [in_vmem(x) for x in inputs]
        before = [in_vmem(b) for b in before]
    args = [*scalars, *inputs, *weights, *before]
    scratch = [
        pltpu.VMEM((utts, kv_rows, cols), jnp.bfloat16),
        pltpu.VMEM((utts, kv_rows, cols), jnp.bfloat16),
        pltpu.VMEM((utts, q_rows, cols), jnp.bfloat16),
        pltpu.VMEM((utts, segs, cols), jnp.float32),
    ]
    in_specs = [smem] * 2
    if first:
        in_specs += [anywhere] + [vmem] * (len(inputs) - 1) + [hbm] * 3
        scratch += [
            pltpu.VMEM((3, feat, cols), jnp.bfloat16),
            pltpu.SemaphoreType.DMA((3 + utts,)),
        ]
    else:
        in_specs += [vmem] * (1 + len(weights))
    in_specs += [vmem] * len(before)
    if last:
        out_specs = [anywhere] * 2
        out_shape = [
            jax.ShapeDtypeStruct((utts, rows, feat), jnp.bfloat16),
            jax.ShapeDtypeStruct((utts, segs, feat), jnp.bfloat16),
        ]
        scratch += [
            pltpu.VMEM(block, jnp.bfloat16),
            pltpu.SemaphoreType.DMA((utts, 2 * len(before) + segs + 1)),
        ]
    else:
        out_specs = [vmem]
        out_shape = [pltpu.VMEM(block, jnp.bfloat16)]
    if first:
        out_specs.append(vmem)
        out_shape.append(pltpu.VMEM((utts, kv_rows + PAD_ROWS, feat), jnp.bfloat16))
    work = 2 * utts * (2 * kv_rows + q_rows) * feat * cols
    return pl.pallas_call(
        make_kernel(dims, first, last, sliced, len(weights), columns, bank_devices, slots),
        in_specs=in_specs,
        out_specs=out_specs,
        out_shape=out_shape,
        scratch_shapes=scratch,
        compiler_params=pltpu.CompilerParams(vmem_limit_bytes=16 * MIB),
        cost_estimate=pl.CostEstimate(
            flops=4 * work, transcendentals=0, bytes_accessed=utts * kv_rows * feat * 2
        ),
        name="attend_first" if first else "attend_next",
    )(*args)


def local(frames_in, memory_in, w_query, w_key, w_value, lengths):
    utts, rows, feat = frames_in.shape
    segs = memory_in.shape[1]
    seg_len = rows // segs
    seq_count = lax.axis_size("seq")
    dp_count = lax.axis_size("dp")
    ids = jnp.stack([lax.axis_index("seq"), lax.axis_index("dp")]).astype(jnp.int32)
    bank_n = segs * seq_count
    part = feat // seq_count
    weights = (w_query, w_key, w_value)
    width = w_query.shape[1]
    sliced = (
        utts == 1
        and len(stage_masks(seq_count)) == 3
        and dp_count & (dp_count - 1) == 0
        and part % LANES == 0
        and width % LANES == 0
        and part * width // feat % PAD_ROWS == 0
        and 4 * segs % PAD_ROWS == 0
        and segs <= PAD_ROWS
        and RIGHT <= LEFT <= rows
    )
    cols = width if sliced else feat // 4
    dims = (utts, rows, feat, cols, segs, seg_len, bank_n)

    if sliced:
        mine, near_sent, far_sent = cut(ids, part, frames_in, memory_in, weights)
        arrived = {0: mine}
        arrived[1] = swapped(mine, "dp", (1, 1))
        near = swapped(near_sent, "seq", (1, 1))
        inner = [(i, i + 1) for i in range(1, seq_count - 1, 2)]
        far = lax.ppermute(far_sent, "seq", inner + [(b, a) for a, b in inner])
        for r in range(2, dp_count):
            low = r & -r
            arrived[r] = swapped(arrived[r ^ low], "dp", (low, low))
        pair_bank = jnp.concatenate([memory_in[0], near[LEFT : LEFT + segs]], axis=0)
        later = []
        for r in range(1, dp_count):
            buffers, slots = gather_slices(arrived[r], "seq", pair_bank if r == 1 else None)
            later.append((("xor", r), slots, buffers))
        own = (("xor", 0), weights)
        edges = (near, far, later[0][2][0], later[0][2][1])
        bank_devices = [(e ^ h, o ^ h) for e, o in later[0][1][:4] for h in (0, 1)]
    else:
        full = [lax.all_gather(w, "dp", axis=1, tiled=True) for w in weights]
        chunks = [
            (("at", c), [w[:, c * cols : (c + 1) * cols] for w in full]) for c in range(feat // cols)
        ]
        own = chunks[0]
        later = [(c, [], [jnp.stack(ws)]) for c, ws in chunks[1:]]
        left = shifted(frames_in[:, rows - LEFT :], "seq", 1)
        right = shifted(frames_in[:, :RIGHT], "seq", -1)
        edges = (left, right, gather_bank(memory_in, "seq"))
        bank_devices = [(t, t) for t in range(seq_count)]

    scalars = (ids, lengths)
    block, x_all = attend_chunk(
        dims,
        sliced,
        True,
        False,
        scalars,
        (frames_in, *edges),
        own[1],
        [own[0]],
        bank_devices,
        [],
    )
    blocks = [block]
    columns = [own[0]]
    for n, (source, slots, buffers) in enumerate(later):
        last = n == len(later) - 1
        columns.append(source)
        outs = attend_chunk(
            dims,
            sliced,
            False,
            last,
            scalars,
            (x_all,),
            buffers,
            list(columns),
            bank_devices,
            slots,
            blocks if last else (),
        )
        blocks.append(outs[0])
    return tuple(outs)


def solution(mesh):
    placed = (
        P("dp", "seq", None),
        P("dp", "seq", None),
        P(None, "dp"),
        P(None, "dp"),
        P(None, "dp"),
        P("dp"),
    )
    return jax.shard_map(
        local,
        mesh=mesh,
        in_specs=placed,
        out_specs=(P("dp", "seq", None), P("dp", "seq", None)),
        check_vma=False,
    )
```

```python
import math

import jax
import jax.numpy as jnp
from jax import lax
from jax.experimental import pallas as pl
from jax.experimental.pallas import tpu as pltpu
from jax.sharding import PartitionSpec as P


HEADS = 16
LEFT = 128
RIGHT = 32
LANES = 128
PAD_ROWS = 16
DEAD = -1e30
MIB = 1024 * 1024


def shifted(block, axis, distance):
    count = lax.axis_size(axis)
    route = [(i - distance, i) for i in range(count) if 0 <= i - distance < count]
    return lax.ppermute(block, axis, route)


def swapped(block, axis, masks):
    count = lax.axis_size(axis)
    return lax.ppermute(block, axis, [(i, i ^ masks[i % 2]) for i in range(count)])


def stage_masks(count):
    bits = [1 << b for b in range(1, count.bit_length() - 1)]
    turned = bits[1:] + bits[:1]
    return [pair for pair in zip(bits, turned)] + [(1, 1)]


def joined(parts):
    rows = sum(p.shape[0] for p in parts)
    out = jnp.zeros((rows,) + parts[0].shape[1:], parts[0].dtype)
    at = 0
    for p in parts:
        out = lax.dynamic_update_slice_in_dim(out, p, at, 0)
        at += p.shape[0]
    return out


def gather_slices(mine, axis, tail=None, got=None):
    (even_a, odd_a), (even_b, odd_b) = stage_masks(lax.axis_size(axis))[:2]
    size = mine.shape[0]
    sent = mine if tail is None else joined([mine, *tail])
    if got is None:
        got = swapped(sent, axis, (even_a, odd_a))
    both = [mine, got] if tail is None else [mine, got[:size], *tail, got[size:]]
    held = joined(both)
    other = swapped(held, axis, (even_b, odd_b))
    pair_held = swapped(held, axis, (1, 1))
    pair_other = swapped(other, axis, (1, 1))
    slots = [(0, 0), (even_a, odd_a), (even_b, odd_b), (even_a ^ even_b, odd_a ^ odd_b)]
    slots += [(o ^ 1, e ^ 1) for e, o in slots]
    return [held, other, pair_held, pair_other], slots, got


def gather_bank(memory_in, axis):
    count = lax.axis_size(axis)
    bank = memory_in
    bit = 1
    while bit < count:
        bank = jnp.concatenate([bank, swapped(bank, axis, (bit, bit))], axis=1)
        bit *= 2
    return bank


def cut(ids, part, frames_in, memory_in, weights):
    _, rows, feat = frames_in.shape
    segs = memory_in.shape[1]
    cols = weights[0].shape[1]
    groups = feat // cols

    def kernel(ids_ref, f_ref, m_ref, *refs):
        w_refs = refs[:3]
        u_ref, near_ref, far_ref, bank_ref, m_scr, sem = refs[3:]
        at = pl.multiple_of(ids_ref[0] * part, part)
        odd = ids_ref[0] % 2
        top = pl.multiple_of((rows - LEFT) * odd, PAD_ROWS)
        end = pl.multiple_of((rows - LEFT) * (1 - odd), PAD_ROWS)
        copies = [pltpu.make_async_copy(m_ref.at[0], m_scr, sem.at[0])]
        copies += [
            pltpu.make_async_copy(
                w.at[pl.ds(at, part)], u_ref.at[pl.ds(n * part, part)], sem.at[1 + n]
            )
            for n, w in enumerate(w_refs)
        ]
        copies += [
            pltpu.make_async_copy(f_ref.at[0, pl.ds(end, LEFT)], near_ref, sem.at[4]),
            pltpu.make_async_copy(f_ref.at[0, pl.ds(top, LEFT)], far_ref, sem.at[5]),
        ]
        for c in copies:
            c.start()
        copies[0].wait()
        folded = [m_scr[:, g * cols : (g + 1) * cols] for g in range(groups)]
        bank_ref[...] = jnp.concatenate(folded, axis=0)
        for c in copies[1:]:
            c.wait()

    hbm = pl.BlockSpec(memory_space=pltpu.HBM)
    vmem = pl.BlockSpec(memory_space=pltpu.VMEM)
    return pl.pallas_call(
        kernel,
        in_specs=[pl.BlockSpec(memory_space=pltpu.SMEM)] + [hbm] * 5,
        out_specs=[vmem] * 4,
        out_shape=[
            jax.ShapeDtypeStruct((3 * part, cols), jnp.bfloat16),
            jax.ShapeDtypeStruct((LEFT, feat), jnp.bfloat16),
            jax.ShapeDtypeStruct((LEFT, feat), jnp.bfloat16),
            jax.ShapeDtypeStruct((groups * segs, cols), jnp.bfloat16),
        ],
        scratch_shapes=[
            pltpu.VMEM((segs, feat), jnp.bfloat16),
            pltpu.SemaphoreType.DMA((6,)),
        ],
        compiler_params=pltpu.CompilerParams(vmem_limit_bytes=4 * MIB),
        name="cut",
    )(ids, *[in_hbm(a) for a in (frames_in, memory_in, *weights)])


def in_hbm(a):
    return pltpu.with_memory_space_constraint(a, pltpu.HBM)


def in_vmem(a):
    return pltpu.with_memory_space_constraint(a, pltpu.VMEM)


def head_lanes(cols, hd):
    return lax.broadcasted_iota(jnp.int32, (1, cols), 1) // hd


def only(a, h, hd):
    return jnp.where(head_lanes(a.shape[1], hd) == h, a, jnp.zeros_like(a))


def split(a):
    return [a[:, j : j + LANES] for j in range(0, a.shape[1], LANES)]


def folded(parts, op):
    out = parts[0]
    for part in parts[1:]:
        out = op(out, part)
    return out


def score_segment(q, k_main, k_tail, hd):
    heads = q.shape[1] // hd
    scale = float(hd) ** (-0.5)
    exact = math.frexp(scale)[0] == 0.5
    if exact:
        q = q * jnp.asarray(scale, q.dtype)
    across = (((1,), (1,)), ((), ()))
    main = lax.dot_general(
        jnp.concatenate([only(q, h, hd) for h in range(heads)], axis=0),
        k_main,
        across,
        preferred_element_type=jnp.float32,
    )
    tail = lax.dot_general(
        q,
        jnp.concatenate([only(k_tail, h, hd) for h in range(heads)], axis=0),
        across,
        preferred_element_type=jnp.float32,
    )
    if not exact:
        main = main * scale
        tail = tail * scale
    return main, tail


def weigh_segment(s_ref, t_ref, p_ref, n_q, heads, tail_n, main_bias, tail_bias):
    main_n = s_ref.shape[1]
    tail_head = lax.broadcasted_iota(jnp.int32, (1, heads * tail_n), 1) // tail_n
    tails = split(t_ref[...] + tail_bias)
    owners = split(tail_head)
    held = [
        [j for j in range(len(tails)) if j * LANES < (h + 1) * tail_n and (j + 1) * LANES > h * tail_n]
        for h in range(heads)
    ]
    tops = []
    sums = []
    for h in range(heads):
        scores = s_ref[h * n_q : (h + 1) * n_q, :] + main_bias
        parts = split(scores) + [jnp.where(owners[j] == h, tails[j], DEAD) for j in held[h]]
        top = jnp.max(folded(parts, jnp.maximum), axis=-1, keepdims=True)
        probs = jnp.exp(scores - top)
        tops.append(top)
        sums.append(folded(split(probs), jnp.add))
        p_ref[:, h * main_n : (h + 1) * main_n] = probs.astype(jnp.bfloat16)
    for j, block in enumerate(tails):
        inside = [h for h in range(heads) if j in held[h]]
        top = tops[inside[0]]
        for h in inside[1:]:
            top = jnp.where(owners[j] >= h, tops[h], top)
        probs = jnp.exp(block - top)
        for h in inside:
            sums[h] = sums[h] + jnp.where(owners[j] == h, probs, 0.0)
        at = heads * main_n + j * LANES
        p_ref[:, at : at + LANES] = probs.astype(jnp.bfloat16)
    return [1.0 / jnp.sum(total, axis=-1, keepdims=True) for total in sums]


def mix_segment(probs, shares, v_main, v_tail, hd):
    heads = v_main.shape[1] // hd
    mixed = jnp.dot(
        probs,
        jnp.concatenate([only(v, h, hd) for v in (v_main, v_tail) for h in range(heads)], axis=0),
        preferred_element_type=jnp.float32,
    )
    outs = []
    for block, head in zip(split(mixed), split(head_lanes(v_main.shape[1], hd))):
        at = len(outs) * LANES
        inside = [h for h in range(heads) if at <= h * hd < at + LANES]
        share = shares[inside[0]]
        for h in inside[1:]:
            share = jnp.where(head >= h, shares[h], share)
        outs.append(block * share)
    return jnp.concatenate(outs, axis=1)


def make_kernel(dims, first, last, sliced, n_buffers, columns, bank_devices, slots):
    utts, rows, feat, cols, segs, seg_len, bank_n = dims
    hd = feat // HEADS
    heads = cols // hd
    main_n = LEFT + seg_len
    tail_n = bank_n + RIGHT
    kv_rows = bank_n + LEFT + rows + RIGHT
    q_base = bank_n + LEFT
    n_slots = len(slots)
    n_before = len(columns) - 1 if last else 0

    def kernel(*refs):
        refs = list(refs)

        def take(n):
            got = refs[:n]
            del refs[:n]
            return got

        ids_ref, len_ref = take(2)
        if first:
            banks = take(2 if sliced else 1)
            _, k_scr, v_scr, q_scr = take(4)
        else:
            (x_ref,) = take(1)
        w_refs = take(n_buffers)
        before = take(n_before)
        if last:
            ctx_ref, mem_ref = take(2)
        else:
            (o_ref,) = take(1)
        if first:
            (x_ref,) = take(1)
        if not first:
            k_scr, v_scr, q_scr = take(3)
        m_scr, s_scr, t_scr, p_scr = take(4)
        k_bank, v_bank = take(2) if first else (k_scr, v_scr)
        if last:
            o_ref, out_sem = take(2)
        seq_index = ids_ref[0]
        odd = seq_index % 2 == 1
        row_base = seq_index * rows
        waits = []

        def column(which):
            kind, value = columns[which]
            index = ids_ref[1] ^ value if kind == "xor" else value
            return pl.multiple_of(index * cols, cols)

        def device(pair):
            return seq_index ^ jnp.where(odd, pair[1], pair[0])

        def write_out(block_ref, at, u, lo, size, target, sem):
            done = pltpu.make_async_copy(
                block_ref.at[u, pl.ds(lo, size)],
                target.at[u, pl.ds(0 if target is mem_ref else lo, size), pl.ds(at, cols)],
                sem,
            )
            done.start()
            waits.append(done)

        for n, block_ref in enumerate(before):
            for u in range(utts):
                write_out(block_ref, column(n), u, 0, rows, ctx_ref, out_sem.at[u, 2 * n])
                write_out(
                    block_ref, column(n), u, rows, segs, mem_ref, out_sem.at[u, 2 * n + 1]
                )

        if first and sliced:
            groups = feat // cols
            blocks = len(bank_devices) // 2
            for n, ref in enumerate(banks):
                top = ref.shape[0] - blocks * groups * segs
                tail = ref[top:, :].astype(jnp.float32)
                for g in range(groups):
                    rows_of = [
                        tail[(b * groups + g) * segs : (b * groups + g + 1) * segs]
                        for b in range(blocks)
                    ]
                    x_ref[
                        0, n * bank_n // 2 : (n + 1) * bank_n // 2, g * cols : (g + 1) * cols
                    ] = jnp.concatenate(rows_of, axis=0).astype(jnp.bfloat16)
        elif first:
            x_ref[:, :bank_n, :] = banks[0][...]

        tail_at = lax.broadcasted_iota(jnp.int32, (1, heads * tail_n), 1) % tail_n
        block = tail_at // segs
        entry = tail_at % segs
        for b, pair in enumerate(bank_devices):
            entry = entry + jnp.where(block == b, device(pair) * segs, 0)
        main_at = lax.broadcasted_iota(jnp.int32, (1, main_n), 1)

        for u in range(utts):
            length = len_ref[u]

            def project(which, lo, hi):
                if first or n_slots == 0:
                    w = w_refs[which - 1][...] if first else w_refs[0][which]
                    return jnp.dot(
                        x_ref[u, lo:hi, :], w, preferred_element_type=jnp.float32
                    ).astype(jnp.bfloat16)
                part = feat // n_slots
                per = n_slots // n_buffers
                acc = None
                for t in range(0, n_slots, 2):
                    lhs = []
                    rhs = []
                    for s in (t, t + 1):
                        at = pl.multiple_of(device(slots[s]) * part, LANES)
                        lhs.append(x_ref[u, lo:hi, pl.ds(at, part)])
                        top = (s % per * 3 + which) * part
                        rhs.append(w_refs[s // per][top : top + part, :])
                    one = jnp.dot(
                        jnp.concatenate(lhs, axis=1),
                        jnp.concatenate(rhs, axis=0),
                        preferred_element_type=jnp.float32,
                    )
                    acc = one if acc is None else acc + one
                return acc.astype(jnp.bfloat16)

            if first:
                k_bank[u] = project(1, 0, bank_n)
                v_bank[u] = project(2, 0, bank_n)
            else:
                k_scr[u] = project(1, 0, kv_rows)
                v_scr[u] = project(2, 0, kv_rows)
                q_scr[u] = project(0, q_base, kv_rows + PAD_ROWS)

            def keys(scr, bank, s):
                win = bank_n + s * seg_len
                edge = win + main_n
                both = [bank[u, :bank_n, :], scr[u, edge : edge + RIGHT, :]]
                return scr[u, win:edge, :], jnp.concatenate(both, axis=0)

            def score(s):
                q = jnp.concatenate(
                    [q_scr[u, s * seg_len : (s + 1) * seg_len, :], q_scr[u, rows + RIGHT :, :]],
                    axis=0,
                )
                s_scr[s % 2], t_scr[s % 2] = score_segment(q, *keys(k_scr, k_bank, s), hd)

            score(0)
            for s in range(segs):
                if s + 1 < segs:
                    score(s + 1)
                seg_index = seq_index * segs + s
                start = row_base + s * seg_len
                main_pos = start - LEFT + main_at
                main_bias = jnp.where((main_pos >= 0) & (main_pos < length), 0.0, DEAD)
                bank_live = (tail_at < bank_n) & (entry < seg_index) & (entry * seg_len < length)
                right_pos = start + seg_len - bank_n + tail_at
                tail_live = bank_live | ((tail_at >= bank_n) & (right_pos < length))
                tail_bias = jnp.where(tail_live, 0.0, DEAD)
                shares = weigh_segment(
                    s_scr.at[s % 2],
                    t_scr.at[s % 2],
                    p_scr.at[s % 2],
                    seg_len + PAD_ROWS,
                    heads,
                    tail_n,
                    main_bias,
                    tail_bias,
                )
                out = mix_segment(p_scr[s % 2], shares, *keys(v_scr, v_bank, s), hd)
                row_at = lax.broadcasted_iota(jnp.int32, (seg_len, 1), 0)
                live = jnp.where(start + row_at < length, out[:seg_len], 0.0)
                o_ref[u, s * seg_len : (s + 1) * seg_len, :] = live.astype(jnp.bfloat16)
                m_scr[u, s : s + 1, :] = out[seg_len + s : seg_len + s + 1]
                if last:
                    write_out(
                        o_ref,
                        column(-1),
                        u,
                        s * seg_len,
                        seg_len,
                        ctx_ref,
                        out_sem.at[u, 2 * n_before + s],
                    )
            o_ref[u, rows : rows + segs, :] = m_scr[u].astype(jnp.bfloat16)
            if last:
                write_out(
                    o_ref, column(-1), u, rows, segs, mem_ref, out_sem.at[u, 2 * n_before + segs]
                )
        for done in waits:
            done.wait()

    return kernel


def prepare(dims, sliced, scalars, frames_in, edges, weights):
    utts, rows, feat, cols, _, seg_len, bank_n = dims
    kv_rows = bank_n + LEFT + rows + RIGHT
    q_base = bank_n + LEFT
    q_rows = rows + RIGHT + PAD_ROWS

    def kernel(ids_ref, len_ref, frames_ref, *refs):
        first_edge, second_edge, wq_ref, wk_ref, wv_ref, x_ref, k_ref, v_ref, q_ref, sem = refs
        seq_index = ids_ref[0]
        odd = seq_index % 2 == 1
        row_base = seq_index * rows
        moves = [
            pltpu.make_async_copy(frames_ref.at[u], x_ref.at[u, pl.ds(q_base, rows)], sem.at[u])
            for u in range(utts)
        ]
        for c in moves:
            c.start()
        if sliced:
            near = first_edge[...]
            far = second_edge[...]
            x_ref[0, bank_n:q_base, :] = jnp.where(odd, near, far)
            x_ref[0, q_base + rows : kv_rows, :] = jnp.where(odd, far[:RIGHT], near[:RIGHT])
        else:
            x_ref[:, bank_n:q_base, :] = first_edge[...]
            x_ref[:, q_base + rows : kv_rows, :] = second_edge[...]
        for c in moves:
            c.wait()
        for u in range(utts):
            length = len_ref[u]
            seg_of = lax.broadcasted_iota(jnp.int32, (PAD_ROWS, rows), 0)
            pos = lax.broadcasted_iota(jnp.int32, (PAD_ROWS, rows), 1)
            pick = (pos // seg_len == seg_of) & (row_base + pos < length)
            sums = jnp.dot(
                jnp.where(pick, 1.0, 0.0).astype(jnp.bfloat16),
                x_ref[u, q_base : q_base + rows, :],
                preferred_element_type=jnp.float32,
            )
            seg = lax.broadcasted_iota(jnp.int32, (PAD_ROWS, 1), 0)
            count = jnp.clip(length - (row_base + seg * seg_len), 1, seg_len)
            mean = sums / count.astype(jnp.float32)
            x_ref[u, kv_rows:, :] = mean.astype(jnp.bfloat16)
            for w_ref, out_ref, lo, hi, at in (
                (wk_ref, k_ref, bank_n, kv_rows, bank_n),
                (wv_ref, v_ref, bank_n, kv_rows, bank_n),
                (wq_ref, q_ref, q_base, kv_rows + PAD_ROWS, 0),
            ):
                out_ref[u, at : at + hi - lo, :] = jnp.dot(
                    x_ref[u, lo:hi, :], w_ref[...], preferred_element_type=jnp.float32
                ).astype(jnp.bfloat16)

    vmem = pl.BlockSpec(memory_space=pltpu.VMEM)
    work = 2 * utts * (2 * kv_rows + q_rows) * feat * cols
    return pl.pallas_call(
        kernel,
        in_specs=[pl.BlockSpec(memory_space=pltpu.SMEM)] * 2
        + [pl.BlockSpec(memory_space=pl.ANY)]
        + [vmem] * 5,
        out_specs=[vmem] * 4,
        out_shape=[
            pltpu.VMEM((utts, kv_rows + PAD_ROWS, feat), jnp.bfloat16),
            pltpu.VMEM((utts, kv_rows, cols), jnp.bfloat16),
            pltpu.VMEM((utts, kv_rows, cols), jnp.bfloat16),
            pltpu.VMEM((utts, q_rows, cols), jnp.bfloat16),
        ],
        scratch_shapes=[pltpu.SemaphoreType.DMA((utts,))],
        compiler_params=pltpu.CompilerParams(vmem_limit_bytes=16 * MIB),
        cost_estimate=pl.CostEstimate(
            flops=4 * work, transcendentals=0, bytes_accessed=utts * kv_rows * feat * 2
        ),
        name="prepare",
    )(*scalars, frames_in, *edges, *weights)


def attend_chunk(
    dims, sliced, first, last, scalars, inputs, weights, columns, bank_devices, slots, before=()
):
    utts, rows, feat, cols, segs, seg_len, bank_n = dims
    kv_rows = bank_n + LEFT + rows + RIGHT
    q_rows = rows + RIGHT + PAD_ROWS
    block = (utts, rows + PAD_ROWS, cols)
    anywhere = pl.BlockSpec(memory_space=pl.ANY)
    vmem = pl.BlockSpec(memory_space=pltpu.VMEM)
    smem = pl.BlockSpec(memory_space=pltpu.SMEM)
    held = [in_vmem(x) for x in (inputs[-4:] if first else inputs)]
    inputs = [*inputs[:-4], *held] if first else held
    before = [in_vmem(b) for b in before]
    args = [*scalars, *inputs, *weights, *before]
    heads = cols * HEADS // feat
    n_q = seg_len + PAD_ROWS
    main_n = LEFT + seg_len
    tail_n = bank_n + RIGHT
    scratch = [
        pltpu.VMEM((utts, segs, cols), jnp.float32),
        pltpu.VMEM((2, heads * n_q, main_n), jnp.float32),
        pltpu.VMEM((2, n_q, heads * tail_n), jnp.float32),
        pltpu.VMEM((2, n_q, heads * (main_n + tail_n)), jnp.bfloat16),
    ]
    if first:
        scratch += [pltpu.VMEM((utts, bank_n, cols), jnp.bfloat16)] * 2
    else:
        scratch = [
            pltpu.VMEM((utts, kv_rows, cols), jnp.bfloat16),
            pltpu.VMEM((utts, kv_rows, cols), jnp.bfloat16),
            pltpu.VMEM((utts, q_rows, cols), jnp.bfloat16),
        ] + scratch
    in_specs = [smem] * 2 + [vmem] * (len(inputs) + len(weights))
    in_specs += [vmem] * len(before)
    aliases = {}
    if last:
        out_specs = [anywhere] * 2
        out_shape = [
            jax.ShapeDtypeStruct((utts, rows, feat), jnp.bfloat16),
            jax.ShapeDtypeStruct((utts, segs, feat), jnp.bfloat16),
        ]
        scratch += [
            pltpu.VMEM(block, jnp.bfloat16),
            pltpu.SemaphoreType.DMA((utts, 2 * len(before) + segs + 1)),
        ]
    else:
        out_specs = [vmem]
        out_shape = [pltpu.VMEM(block, jnp.bfloat16)]
    if first:
        out_specs.append(vmem)
        out_shape.append(pltpu.VMEM((utts, kv_rows + PAD_ROWS, feat), jnp.bfloat16))
        aliases = {2 + len(inputs) - 4: 1}
    work = 2 * utts * (2 * kv_rows + q_rows) * feat * cols
    return pl.pallas_call(
        make_kernel(dims, first, last, sliced, len(weights), columns, bank_devices, slots),
        in_specs=in_specs,
        out_specs=out_specs,
        out_shape=out_shape,
        scratch_shapes=scratch,
        input_output_aliases=aliases,
        compiler_params=pltpu.CompilerParams(vmem_limit_bytes=16 * MIB),
        cost_estimate=pl.CostEstimate(
            flops=4 * work, transcendentals=0, bytes_accessed=utts * kv_rows * feat * 2
        ),
        name="attend_first" if first else "attend_next",
    )(*args)


def local(frames_in, memory_in, w_query, w_key, w_value, lengths):
    utts, rows, feat = frames_in.shape
    segs = memory_in.shape[1]
    seg_len = rows // segs
    seq_count = lax.axis_size("seq")
    dp_count = lax.axis_size("dp")
    ids = jnp.stack([lax.axis_index("seq"), lax.axis_index("dp")]).astype(jnp.int32)
    bank_n = segs * seq_count
    part = feat // seq_count
    weights = (w_query, w_key, w_value)
    width = w_query.shape[1]
    sliced = (
        utts == 1
        and len(stage_masks(seq_count)) == 3
        and dp_count & (dp_count - 1) == 0
        and part % LANES == 0
        and width % LANES == 0
        and feat // width * segs % PAD_ROWS == 0
        and 4 * segs % PAD_ROWS == 0
        and RIGHT <= LEFT <= rows
    )
    cols = width if sliced else feat // 4
    dims = (utts, rows, feat, cols, segs, seg_len, bank_n)

    if sliced:
        mine, near_sent, far_sent, own_bank = cut(ids, part, frames_in, memory_in, weights)
        arrived = {0: mine}
        arrived[1] = swapped(mine, "dp", (1, 1))
        pair_bank = [own_bank, swapped(own_bank, "seq", (1, 1))]
        near = swapped(near_sent, "seq", (1, 1))
        inner = [(i, i + 1) for i in range(1, seq_count - 1, 2)]
        far = lax.ppermute(far_sent, "seq", inner + [(b, a) for a, b in inner])
        for r in range(2, dp_count):
            low = r & -r
            arrived[r] = swapped(arrived[r ^ low], "dp", (low, low))
        later = []
        firsts = {}
        for r in range(1, dp_count):
            low = r & -r
            if r != low:
                firsts[r] = swapped(firsts[r ^ low], "dp", (low, low))
            buffers, slots, firsts[r] = gather_slices(
                arrived[r], "seq", pair_bank if r == 1 else None, firsts.get(r)
            )
            later.append((("xor", r), slots, buffers))
        own = (("xor", 0), weights)
        edges = (near, far)
        banks = tuple(later[0][2][:2])
        bank_devices = [(e ^ h, o ^ h) for e, o in later[0][1][:4] for h in (0, 1)]
    else:
        full = [lax.all_gather(w, "dp", axis=1, tiled=True) for w in weights]
        chunks = [
            (("at", c), [w[:, c * cols : (c + 1) * cols] for w in full]) for c in range(feat // cols)
        ]
        own = chunks[0]
        later = [(c, [], [jnp.stack(ws)]) for c, ws in chunks[1:]]
        left = shifted(frames_in[:, rows - LEFT :], "seq", 1)
        right = shifted(frames_in[:, :RIGHT], "seq", -1)
        edges = (left, right)
        banks = (gather_bank(memory_in, "seq"),)
        bank_devices = [(t, t) for t in range(seq_count)]

    scalars = (ids, lengths)
    prepared = prepare(dims, sliced, scalars, frames_in, edges, own[1])
    block, x_all = attend_chunk(
        dims,
        sliced,
        True,
        False,
        scalars,
        (*banks, *prepared),
        own[1][1:],
        [own[0]],
        bank_devices,
        [],
    )
    blocks = [block]
    columns = [own[0]]
    for n, (source, slots, buffers) in enumerate(later):
        last = n == len(later) - 1
        columns.append(source)
        outs = attend_chunk(
            dims,
            sliced,
            False,
            last,
            scalars,
            (x_all,),
            buffers,
            list(columns),
            bank_devices,
            slots,
            blocks if last else (),
        )
        blocks.append(outs[0])
    return tuple(outs)


def solution(mesh):
    placed = (
        P("dp", "seq", None),
        P("dp", "seq", None),
        P(None, "dp"),
        P(None, "dp"),
        P(None, "dp"),
        P("dp"),
    )
    return jax.shard_map(
        local,
        mesh=mesh,
        in_specs=placed,
        out_specs=(P("dp", "seq", None), P("dp", "seq", None)),
        check_vma=False,
    )
```

```python
import math

import jax
import jax.numpy as jnp
from jax import lax
from jax.experimental import pallas as pl
from jax.experimental.pallas import tpu as pltpu
from jax.sharding import PartitionSpec as P


HEADS = 16
LEFT = 128
RIGHT = 32
LANES = 128
PAD_ROWS = 16
DEAD = -1e30
MIB = 1024 * 1024


def shifted(block, axis, distance):
    count = lax.axis_size(axis)
    route = [(i - distance, i) for i in range(count) if 0 <= i - distance < count]
    return lax.ppermute(block, axis, route)


def swapped(block, axis, masks):
    count = lax.axis_size(axis)
    return lax.ppermute(block, axis, [(i, i ^ masks[i % 2]) for i in range(count)])


def stage_masks(count):
    bits = [1 << b for b in range(1, count.bit_length() - 1)]
    turned = bits[1:] + bits[:1]
    return [pair for pair in zip(bits, turned)] + [(1, 1)]


def joined(parts):
    rows = sum(p.shape[0] for p in parts)
    out = jnp.zeros((rows,) + parts[0].shape[1:], parts[0].dtype)
    at = 0
    for p in parts:
        out = lax.dynamic_update_slice_in_dim(out, p, at, 0)
        at += p.shape[0]
    return out


def gather_slices(mine, axis, tail=None, got=None):
    (even_a, odd_a), (even_b, odd_b) = stage_masks(lax.axis_size(axis))[:2]
    size = mine.shape[0]
    if got is not None:
        blocks = [mine, got]
        for n in range(2):
            blocks.append(swapped(blocks[n], axis, (even_b, odd_b)))
        for n in range(4):
            blocks.append(swapped(blocks[n], axis, (1, 1)))
        slots = [(0, 0), (even_a, odd_a), (even_b, odd_b), (even_a ^ even_b, odd_a ^ odd_b)]
        slots += [(o ^ 1, e ^ 1) for e, o in slots]
        return blocks, slots, got
    sent = mine if tail is None else joined([mine, *tail])
    if got is None:
        got = swapped(sent, axis, (even_a, odd_a))
    both = [mine, got] if tail is None else [mine, got[:size], *tail, got[size:]]
    held = joined(both)
    other = swapped(held, axis, (even_b, odd_b))
    pair_held = swapped(held, axis, (1, 1))
    pair_other = swapped(other, axis, (1, 1))
    slots = [(0, 0), (even_a, odd_a), (even_b, odd_b), (even_a ^ even_b, odd_a ^ odd_b)]
    slots += [(o ^ 1, e ^ 1) for e, o in slots]
    return [held, other, pair_held, pair_other], slots, got


def gather_bank(memory_in, axis):
    count = lax.axis_size(axis)
    bank = memory_in
    bit = 1
    while bit < count:
        bank = jnp.concatenate([bank, swapped(bank, axis, (bit, bit))], axis=1)
        bit *= 2
    return bank


def cut(ids, part, frames_in, memory_in, weights):
    _, rows, feat = frames_in.shape
    segs = memory_in.shape[1]
    cols = weights[0].shape[1]
    groups = feat // cols

    def kernel(ids_ref, f_ref, m_ref, *refs):
        w_refs = refs[:3]
        u_ref, near_ref, far_ref, bank_ref, m_scr, sem = refs[3:]
        at = pl.multiple_of(ids_ref[0] * part, part)
        odd = ids_ref[0] % 2
        top = pl.multiple_of((rows - LEFT) * odd, PAD_ROWS)
        end = pl.multiple_of((rows - LEFT) * (1 - odd), PAD_ROWS)
        copies = [pltpu.make_async_copy(m_ref.at[0], m_scr, sem.at[0])]
        copies += [
            pltpu.make_async_copy(
                w.at[pl.ds(at, part)], u_ref.at[pl.ds(n * part, part)], sem.at[1 + n]
            )
            for n, w in enumerate(w_refs)
        ]
        copies += [
            pltpu.make_async_copy(f_ref.at[0, pl.ds(end, LEFT)], near_ref, sem.at[4]),
            pltpu.make_async_copy(f_ref.at[0, pl.ds(top, LEFT)], far_ref, sem.at[5]),
        ]
        for c in copies:
            c.start()
        copies[0].wait()
        folded = [m_scr[:, g * cols : (g + 1) * cols] for g in range(groups)]
        bank_ref[...] = jnp.concatenate(folded, axis=0)
        for c in copies[1:]:
            c.wait()

    hbm = pl.BlockSpec(memory_space=pltpu.HBM)
    vmem = pl.BlockSpec(memory_space=pltpu.VMEM)
    return pl.pallas_call(
        kernel,
        in_specs=[pl.BlockSpec(memory_space=pltpu.SMEM)] + [hbm] * 5,
        out_specs=[vmem] * 4,
        out_shape=[
            jax.ShapeDtypeStruct((3 * part, cols), jnp.bfloat16),
            jax.ShapeDtypeStruct((LEFT, feat), jnp.bfloat16),
            jax.ShapeDtypeStruct((LEFT, feat), jnp.bfloat16),
            jax.ShapeDtypeStruct((groups * segs, cols), jnp.bfloat16),
        ],
        scratch_shapes=[
            pltpu.VMEM((segs, feat), jnp.bfloat16),
            pltpu.SemaphoreType.DMA((6,)),
        ],
        compiler_params=pltpu.CompilerParams(vmem_limit_bytes=4 * MIB),
        name="cut",
    )(ids, *[in_hbm(a) for a in (frames_in, memory_in, *weights)])


def in_hbm(a):
    return pltpu.with_memory_space_constraint(a, pltpu.HBM)


def in_vmem(a):
    return pltpu.with_memory_space_constraint(a, pltpu.VMEM)


def head_lanes(cols, hd):
    return lax.broadcasted_iota(jnp.int32, (1, cols), 1) // hd


def only(a, h, hd):
    return jnp.where(head_lanes(a.shape[1], hd) == h, a, jnp.zeros_like(a))


def split(a):
    return [a[:, j : j + LANES] for j in range(0, a.shape[1], LANES)]


def folded(parts, op):
    out = parts[0]
    for part in parts[1:]:
        out = op(out, part)
    return out


def score_segment(q, k_main, k_tail, hd):
    heads = q.shape[1] // hd
    scale = float(hd) ** (-0.5)
    exact = math.frexp(scale)[0] == 0.5
    if exact:
        q = q * jnp.asarray(scale, q.dtype)
    across = (((1,), (1,)), ((), ()))
    main = lax.dot_general(
        jnp.concatenate([only(q, h, hd) for h in range(heads)], axis=0),
        k_main,
        across,
        preferred_element_type=jnp.float32,
    )
    tail = lax.dot_general(
        q,
        jnp.concatenate([only(k_tail, h, hd) for h in range(heads)], axis=0),
        across,
        preferred_element_type=jnp.float32,
    )
    if not exact:
        main = main * scale
        tail = tail * scale
    return main, tail


def weigh_segment(s_ref, t_ref, p_ref, n_q, heads, tail_n, main_bias, tail_bias):
    main_n = s_ref.shape[1]
    tail_head = lax.broadcasted_iota(jnp.int32, (1, heads * tail_n), 1) // tail_n
    tails = split(t_ref[...] + tail_bias)
    owners = split(tail_head)
    held = [
        [j for j in range(len(tails)) if j * LANES < (h + 1) * tail_n and (j + 1) * LANES > h * tail_n]
        for h in range(heads)
    ]
    tops = []
    sums = []
    for h in range(heads):
        scores = s_ref[h * n_q : (h + 1) * n_q, :] + main_bias
        parts = split(scores) + [jnp.where(owners[j] == h, tails[j], DEAD) for j in held[h]]
        top = jnp.max(folded(parts, jnp.maximum), axis=-1, keepdims=True)
        probs = jnp.exp(scores - top)
        tops.append(top)
        sums.append(folded(split(probs), jnp.add))
        p_ref[:, h * main_n : (h + 1) * main_n] = probs.astype(jnp.bfloat16)
    for j, block in enumerate(tails):
        inside = [h for h in range(heads) if j in held[h]]
        top = tops[inside[0]]
        for h in inside[1:]:
            top = jnp.where(owners[j] >= h, tops[h], top)
        probs = jnp.exp(block - top)
        for h in inside:
            sums[h] = sums[h] + jnp.where(owners[j] == h, probs, 0.0)
        at = heads * main_n + j * LANES
        p_ref[:, at : at + LANES] = probs.astype(jnp.bfloat16)
    return [1.0 / jnp.sum(total, axis=-1, keepdims=True) for total in sums]


def mix_segment(probs, shares, v_main, v_tail, hd):
    heads = v_main.shape[1] // hd
    mixed = jnp.dot(
        probs,
        jnp.concatenate([only(v, h, hd) for v in (v_main, v_tail) for h in range(heads)], axis=0),
        preferred_element_type=jnp.float32,
    )
    outs = []
    for block, head in zip(split(mixed), split(head_lanes(v_main.shape[1], hd))):
        at = len(outs) * LANES
        inside = [h for h in range(heads) if at <= h * hd < at + LANES]
        share = shares[inside[0]]
        for h in inside[1:]:
            share = jnp.where(head >= h, shares[h], share)
        outs.append(block * share)
    return jnp.concatenate(outs, axis=1)


def make_kernel(dims, first, last, sliced, n_buffers, columns, bank_devices, slots):
    utts, rows, feat, cols, segs, seg_len, bank_n = dims
    hd = feat // HEADS
    heads = cols // hd
    main_n = LEFT + seg_len
    tail_n = bank_n + RIGHT
    kv_rows = bank_n + LEFT + rows + RIGHT
    q_base = bank_n + LEFT
    n_slots = len(slots)
    n_before = len(columns) - 1 if last else 0

    def kernel(*refs):
        refs = list(refs)

        def take(n):
            got = refs[:n]
            del refs[:n]
            return got

        ids_ref, len_ref = take(2)
        if first:
            banks = take(2 if sliced else 1)
            _, k_scr, v_scr, q_scr = take(4)
        else:
            (x_ref,) = take(1)
        w_refs = take(n_buffers)
        before = take(n_before)
        if last:
            ctx_ref, mem_ref = take(2)
        else:
            (o_ref,) = take(1)
        if first:
            (x_ref,) = take(1)
        if not first:
            k_scr, v_scr, q_scr = take(3)
        m_scr, s_scr, t_scr, p_scr = take(4)
        k_bank, v_bank = take(2) if first else (k_scr, v_scr)
        if last:
            o_ref, out_sem = take(2)
        seq_index = ids_ref[0]
        odd = seq_index % 2 == 1
        row_base = seq_index * rows
        waits = []

        def column(which):
            kind, value = columns[which]
            index = ids_ref[1] ^ value if kind == "xor" else value
            return pl.multiple_of(index * cols, cols)

        def device(pair):
            return seq_index ^ jnp.where(odd, pair[1], pair[0])

        def write_out(block_ref, at, u, lo, size, target, sem):
            done = pltpu.make_async_copy(
                block_ref.at[u, pl.ds(lo, size)],
                target.at[u, pl.ds(0 if target is mem_ref else lo, size), pl.ds(at, cols)],
                sem,
            )
            done.start()
            waits.append(done)

        for n, block_ref in enumerate(before):
            for u in range(utts):
                write_out(block_ref, column(n), u, 0, rows, ctx_ref, out_sem.at[u, 2 * n])
                write_out(
                    block_ref, column(n), u, rows, segs, mem_ref, out_sem.at[u, 2 * n + 1]
                )

        if first and sliced:
            groups = feat // cols
            blocks = len(bank_devices) // 2
            for n, ref in enumerate(banks):
                top = ref.shape[0] - blocks * groups * segs
                tail = ref[top:, :].astype(jnp.float32)
                for g in range(groups):
                    rows_of = [
                        tail[(b * groups + g) * segs : (b * groups + g + 1) * segs]
                        for b in range(blocks)
                    ]
                    x_ref[
                        0, n * bank_n // 2 : (n + 1) * bank_n // 2, g * cols : (g + 1) * cols
                    ] = jnp.concatenate(rows_of, axis=0).astype(jnp.bfloat16)
        elif first:
            x_ref[:, :bank_n, :] = banks[0][...]

        tail_at = lax.broadcasted_iota(jnp.int32, (1, heads * tail_n), 1) % tail_n
        block = tail_at // segs
        entry = tail_at % segs
        for b, pair in enumerate(bank_devices):
            entry = entry + jnp.where(block == b, device(pair) * segs, 0)
        main_at = lax.broadcasted_iota(jnp.int32, (1, main_n), 1)

        for u in range(utts):
            length = len_ref[u]

            def project(which, lo, hi):
                if first or n_slots == 0:
                    w = w_refs[which - 1][...] if first else w_refs[0][which]
                    return jnp.dot(
                        x_ref[u, lo:hi, :], w, preferred_element_type=jnp.float32
                    ).astype(jnp.bfloat16)
                part = feat // n_slots
                places = [
                    (ref, n * 3 * part)
                    for ref in w_refs
                    for n in range(ref.shape[0] // (3 * part))
                ]
                acc = None
                for t in range(0, n_slots, 2):
                    lhs = []
                    rhs = []
                    for s in (t, t + 1):
                        at = pl.multiple_of(device(slots[s]) * part, LANES)
                        lhs.append(x_ref[u, lo:hi, pl.ds(at, part)])
                        ref, top = places[s]
                        rhs.append(ref[top + which * part : top + (which + 1) * part, :])
                    one = jnp.dot(
                        jnp.concatenate(lhs, axis=1),
                        jnp.concatenate(rhs, axis=0),
                        preferred_element_type=jnp.float32,
                    )
                    acc = one if acc is None else acc + one
                return acc.astype(jnp.bfloat16)

            if first:
                k_bank[u] = project(1, 0, bank_n)
                v_bank[u] = project(2, 0, bank_n)
            else:
                k_scr[u] = project(1, 0, kv_rows)
                v_scr[u] = project(2, 0, kv_rows)
                q_scr[u] = project(0, q_base, kv_rows + PAD_ROWS)

            def keys(scr, bank, s):
                win = bank_n + s * seg_len
                edge = win + main_n
                both = [bank[u, :bank_n, :], scr[u, edge : edge + RIGHT, :]]
                return scr[u, win:edge, :], jnp.concatenate(both, axis=0)

            def score(s):
                q = jnp.concatenate(
                    [q_scr[u, s * seg_len : (s + 1) * seg_len, :], q_scr[u, rows + RIGHT :, :]],
                    axis=0,
                )
                s_scr[s % 2], t_scr[s % 2] = score_segment(q, *keys(k_scr, k_bank, s), hd)

            score(0)
            for s in range(segs):
                if s + 1 < segs:
                    score(s + 1)
                seg_index = seq_index * segs + s
                start = row_base + s * seg_len
                main_pos = start - LEFT + main_at
                main_bias = jnp.where((main_pos >= 0) & (main_pos < length), 0.0, DEAD)
                bank_live = (tail_at < bank_n) & (entry < seg_index) & (entry * seg_len < length)
                right_pos = start + seg_len - bank_n + tail_at
                tail_live = bank_live | ((tail_at >= bank_n) & (right_pos < length))
                tail_bias = jnp.where(tail_live, 0.0, DEAD)
                shares = weigh_segment(
                    s_scr.at[s % 2],
                    t_scr.at[s % 2],
                    p_scr.at[s % 2],
                    seg_len + PAD_ROWS,
                    heads,
                    tail_n,
                    main_bias,
                    tail_bias,
                )
                out = mix_segment(p_scr[s % 2], shares, *keys(v_scr, v_bank, s), hd)
                row_at = lax.broadcasted_iota(jnp.int32, (seg_len, 1), 0)
                live = jnp.where(start + row_at < length, out[:seg_len], 0.0)
                o_ref[u, s * seg_len : (s + 1) * seg_len, :] = live.astype(jnp.bfloat16)
                m_scr[u, s : s + 1, :] = out[seg_len + s : seg_len + s + 1]
                if last:
                    write_out(
                        o_ref,
                        column(-1),
                        u,
                        s * seg_len,
                        seg_len,
                        ctx_ref,
                        out_sem.at[u, 2 * n_before + s],
                    )
            o_ref[u, rows : rows + segs, :] = m_scr[u].astype(jnp.bfloat16)
            if last:
                write_out(
                    o_ref, column(-1), u, rows, segs, mem_ref, out_sem.at[u, 2 * n_before + segs]
                )
        for done in waits:
            done.wait()

    return kernel


def prepare(dims, sliced, scalars, frames_in, edges, weights):
    utts, rows, feat, cols, _, seg_len, bank_n = dims
    kv_rows = bank_n + LEFT + rows + RIGHT
    q_base = bank_n + LEFT
    q_rows = rows + RIGHT + PAD_ROWS

    def kernel(ids_ref, len_ref, frames_ref, *refs):
        first_edge, second_edge, wq_ref, wk_ref, wv_ref, x_ref, k_ref, v_ref, q_ref, sem = refs
        seq_index = ids_ref[0]
        odd = seq_index % 2 == 1
        row_base = seq_index * rows
        moves = [
            pltpu.make_async_copy(frames_ref.at[u], x_ref.at[u, pl.ds(q_base, rows)], sem.at[u])
            for u in range(utts)
        ]
        for c in moves:
            c.start()
        if sliced:
            near = first_edge[...]
            far = second_edge[...]
            x_ref[0, bank_n:q_base, :] = jnp.where(odd, near, far)
            x_ref[0, q_base + rows : kv_rows, :] = jnp.where(odd, far[:RIGHT], near[:RIGHT])
        else:
            x_ref[:, bank_n:q_base, :] = first_edge[...]
            x_ref[:, q_base + rows : kv_rows, :] = second_edge[...]
        for c in moves:
            c.wait()
        for u in range(utts):
            length = len_ref[u]
            seg_of = lax.broadcasted_iota(jnp.int32, (PAD_ROWS, rows), 0)
            pos = lax.broadcasted_iota(jnp.int32, (PAD_ROWS, rows), 1)
            pick = (pos // seg_len == seg_of) & (row_base + pos < length)
            sums = jnp.dot(
                jnp.where(pick, 1.0, 0.0).astype(jnp.bfloat16),
                x_ref[u, q_base : q_base + rows, :],
                preferred_element_type=jnp.float32,
            )
            seg = lax.broadcasted_iota(jnp.int32, (PAD_ROWS, 1), 0)
            count = jnp.clip(length - (row_base + seg * seg_len), 1, seg_len)
            mean = sums / count.astype(jnp.float32)
            x_ref[u, kv_rows:, :] = mean.astype(jnp.bfloat16)
            for w_ref, out_ref, lo, hi, at in (
                (wk_ref, k_ref, bank_n, kv_rows, bank_n),
                (wv_ref, v_ref, bank_n, kv_rows, bank_n),
                (wq_ref, q_ref, q_base, kv_rows + PAD_ROWS, 0),
            ):
                out_ref[u, at : at + hi - lo, :] = jnp.dot(
                    x_ref[u, lo:hi, :], w_ref[...], preferred_element_type=jnp.float32
                ).astype(jnp.bfloat16)

    vmem = pl.BlockSpec(memory_space=pltpu.VMEM)
    work = 2 * utts * (2 * kv_rows + q_rows) * feat * cols
    return pl.pallas_call(
        kernel,
        in_specs=[pl.BlockSpec(memory_space=pltpu.SMEM)] * 2
        + [pl.BlockSpec(memory_space=pl.ANY)]
        + [vmem] * 5,
        out_specs=[vmem] * 4,
        out_shape=[
            pltpu.VMEM((utts, kv_rows + PAD_ROWS, feat), jnp.bfloat16),
            pltpu.VMEM((utts, kv_rows, cols), jnp.bfloat16),
            pltpu.VMEM((utts, kv_rows, cols), jnp.bfloat16),
            pltpu.VMEM((utts, q_rows, cols), jnp.bfloat16),
        ],
        scratch_shapes=[pltpu.SemaphoreType.DMA((utts,))],
        compiler_params=pltpu.CompilerParams(vmem_limit_bytes=16 * MIB),
        cost_estimate=pl.CostEstimate(
            flops=4 * work, transcendentals=0, bytes_accessed=utts * kv_rows * feat * 2
        ),
        name="prepare",
    )(*scalars, frames_in, *edges, *weights)


def attend_chunk(
    dims, sliced, first, last, scalars, inputs, weights, columns, bank_devices, slots, before=()
):
    utts, rows, feat, cols, segs, seg_len, bank_n = dims
    kv_rows = bank_n + LEFT + rows + RIGHT
    q_rows = rows + RIGHT + PAD_ROWS
    block = (utts, rows + PAD_ROWS, cols)
    anywhere = pl.BlockSpec(memory_space=pl.ANY)
    vmem = pl.BlockSpec(memory_space=pltpu.VMEM)
    smem = pl.BlockSpec(memory_space=pltpu.SMEM)
    held = [in_vmem(x) for x in (inputs[-4:] if first else inputs)]
    inputs = [*inputs[:-4], *held] if first else held
    before = [in_vmem(b) for b in before]
    args = [*scalars, *inputs, *weights, *before]
    heads = cols * HEADS // feat
    n_q = seg_len + PAD_ROWS
    main_n = LEFT + seg_len
    tail_n = bank_n + RIGHT
    scratch = [
        pltpu.VMEM((utts, segs, cols), jnp.float32),
        pltpu.VMEM((2, heads * n_q, main_n), jnp.float32),
        pltpu.VMEM((2, n_q, heads * tail_n), jnp.float32),
        pltpu.VMEM((2, n_q, heads * (main_n + tail_n)), jnp.bfloat16),
    ]
    if first:
        scratch += [pltpu.VMEM((utts, bank_n, cols), jnp.bfloat16)] * 2
    else:
        scratch = [
            pltpu.VMEM((utts, kv_rows, cols), jnp.bfloat16),
            pltpu.VMEM((utts, kv_rows, cols), jnp.bfloat16),
            pltpu.VMEM((utts, q_rows, cols), jnp.bfloat16),
        ] + scratch
    in_specs = [smem] * 2 + [vmem] * (len(inputs) + len(weights))
    in_specs += [vmem] * len(before)
    aliases = {}
    if last:
        out_specs = [anywhere] * 2
        out_shape = [
            jax.ShapeDtypeStruct((utts, rows, feat), jnp.bfloat16),
            jax.ShapeDtypeStruct((utts, segs, feat), jnp.bfloat16),
        ]
        scratch += [
            pltpu.VMEM(block, jnp.bfloat16),
            pltpu.SemaphoreType.DMA((utts, 2 * len(before) + segs + 1)),
        ]
    else:
        out_specs = [vmem]
        out_shape = [pltpu.VMEM(block, jnp.bfloat16)]
    if first:
        out_specs.append(vmem)
        out_shape.append(pltpu.VMEM((utts, kv_rows + PAD_ROWS, feat), jnp.bfloat16))
        aliases = {2 + len(inputs) - 4: 1}
    work = 2 * utts * (2 * kv_rows + q_rows) * feat * cols
    return pl.pallas_call(
        make_kernel(dims, first, last, sliced, len(weights), columns, bank_devices, slots),
        in_specs=in_specs,
        out_specs=out_specs,
        out_shape=out_shape,
        scratch_shapes=scratch,
        input_output_aliases=aliases,
        compiler_params=pltpu.CompilerParams(vmem_limit_bytes=16 * MIB),
        cost_estimate=pl.CostEstimate(
            flops=4 * work, transcendentals=0, bytes_accessed=utts * kv_rows * feat * 2
        ),
        name="attend_first" if first else "attend_next",
    )(*args)


def local(frames_in, memory_in, w_query, w_key, w_value, lengths):
    utts, rows, feat = frames_in.shape
    segs = memory_in.shape[1]
    seg_len = rows // segs
    seq_count = lax.axis_size("seq")
    dp_count = lax.axis_size("dp")
    ids = jnp.stack([lax.axis_index("seq"), lax.axis_index("dp")]).astype(jnp.int32)
    bank_n = segs * seq_count
    part = feat // seq_count
    weights = (w_query, w_key, w_value)
    width = w_query.shape[1]
    sliced = (
        utts == 1
        and len(stage_masks(seq_count)) == 3
        and dp_count & (dp_count - 1) == 0
        and part % LANES == 0
        and width % LANES == 0
        and feat // width * segs % PAD_ROWS == 0
        and 4 * segs % PAD_ROWS == 0
        and RIGHT <= LEFT <= rows
    )
    cols = width if sliced else feat // 4
    dims = (utts, rows, feat, cols, segs, seg_len, bank_n)

    if sliced:
        mine, near_sent, far_sent, own_bank = cut(ids, part, frames_in, memory_in, weights)
        arrived = {0: mine}
        arrived[1] = swapped(mine, "dp", (1, 1))
        pair_bank = [own_bank, swapped(own_bank, "seq", (1, 1))]
        near = swapped(near_sent, "seq", (1, 1))
        inner = [(i, i + 1) for i in range(1, seq_count - 1, 2)]
        far = lax.ppermute(far_sent, "seq", inner + [(b, a) for a, b in inner])
        for r in range(2, dp_count):
            low = r & -r
            arrived[r] = swapped(arrived[r ^ low], "dp", (low, low))
        later = []
        firsts = {}
        for r in range(1, dp_count):
            low = r & -r
            if r != low:
                firsts[r] = swapped(firsts[r ^ low], "dp", (low, low))
            buffers, slots, firsts[r] = gather_slices(
                arrived[r], "seq", pair_bank if r == 1 else None, firsts.get(r)
            )
            later.append((("xor", r), slots, buffers))
        own = (("xor", 0), weights)
        edges = (near, far)
        banks = tuple(later[0][2][:2])
        bank_devices = [(e ^ h, o ^ h) for e, o in later[0][1][:4] for h in (0, 1)]
    else:
        full = [lax.all_gather(w, "dp", axis=1, tiled=True) for w in weights]
        chunks = [
            (("at", c), [w[:, c * cols : (c + 1) * cols] for w in full]) for c in range(feat // cols)
        ]
        own = chunks[0]
        later = [(c, [], [jnp.stack(ws)]) for c, ws in chunks[1:]]
        left = shifted(frames_in[:, rows - LEFT :], "seq", 1)
        right = shifted(frames_in[:, :RIGHT], "seq", -1)
        edges = (left, right)
        banks = (gather_bank(memory_in, "seq"),)
        bank_devices = [(t, t) for t in range(seq_count)]

    scalars = (ids, lengths)
    prepared = prepare(dims, sliced, scalars, frames_in, edges, own[1])
    block, x_all = attend_chunk(
        dims,
        sliced,
        True,
        False,
        scalars,
        (*banks, *prepared),
        own[1][1:],
        [own[0]],
        bank_devices,
        [],
    )
    blocks = [block]
    columns = [own[0]]
    for n, (source, slots, buffers) in enumerate(later):
        last = n == len(later) - 1
        columns.append(source)
        outs = attend_chunk(
            dims,
            sliced,
            False,
            last,
            scalars,
            (x_all,),
            buffers,
            list(columns),
            bank_devices,
            slots,
            blocks if last else (),
        )
        blocks.append(outs[0])
    return tuple(outs)


def solution(mesh):
    placed = (
        P("dp", "seq", None),
        P("dp", "seq", None),
        P(None, "dp"),
        P(None, "dp"),
        P(None, "dp"),
        P("dp"),
    )
    return jax.shard_map(
        local,
        mesh=mesh,
        in_specs=placed,
        out_specs=(P("dp", "seq", None), P("dp", "seq", None)),
        check_vma=False,
    )
```
